256 devices in a mesh: inp: 8 (over x, core), out: 32 (over z, y).
Axes of the slice: x: 4, y: 4, z: 8, core: 2. Of those that a mesh axis runs over, the one named last changes fastest.
Arguments:
- attention: bfloat16 [128, 16384], P(None, ('inp', 'out')), may hold values from -6 to 6
- residual: bfloat16 [128, 16384], P(None, 'out'), may hold values from -60 to 60
- wo_codes: int32 [2, 2048, 16384], P(None, 'inp', 'out'), may hold values from 0 to 255
- wo_books: bfloat16 [2, 256, 8], replicated, may hold values from -0.03125 to 0.03125
- wo_scale: float32 [16384], P('out'), may hold values from 0.5 to 2
- norm_gain: float32 [16384], replicated, may hold values from 0.25 to 1.75
- gate_codes: int32 [2, 2048, 53248], P(None, 'inp', 'out'), may hold values from 0 to 255
- gate_books: bfloat16 [2, 256, 8], replicated, may hold values from -0.03125 to 0.03125
- gate_scale: float32 [53248], P('out'), may hold values from 0.5 to 2
Outputs:
- stream: bfloat16 [128, 16384], P(None, 'out')
- gate_out: bfloat16 [128, 53248], P('inp', 'out')
The draws below stay inside these ranges and needn't reach their ends.
All inputs are finite; a program needn't handle non-finite values.
Results may differ from the reference program's by a relative error of at most 0.0059.
Values may be sent and summed in bfloat16 or wider, within the bound.
A program may use at most 64 MiB of HBM per device.

```python
import math
import jax
import jax.numpy as jnp
from jax import lax

D = 16384
FF = 53248
B = 128
BOOK = 256
GROUP = 8


def draw_residual(key, part):
    key_row, key_col, key_val = jax.random.split(key, 3)
    position = jnp.linspace(0.0, 1.0, D, dtype=jnp.float32)[None, :]
    rough = jax.random.uniform(key_col, (1, D), jnp.float32, 0.5, 1.5)
    row_scale = jnp.exp(jax.random.uniform(key_row, (B, 1), jnp.float32, jnp.log(0.3), jnp.log(3.0)))
    ramp = jnp.exp(position * jnp.log(3.0))
    values = jnp.clip(jax.random.normal(key_val, (B, D), jnp.float32), -6.0, 6.0)
    result = jnp.clip(values * row_scale * ramp * rough, -60.0, 60.0)
    return result.astype(jnp.bfloat16)


def with_ends(drawn, rng, low, top_value):
    extent = drawn.shape
    index_at = [jax.random.randint(jax.random.fold_in(rng, axis), (), 0, extent[axis]) for axis in range(len(extent))]
    drawn = drawn.at[tuple(index_at)].set(low)
    longest = extent.index(max(extent))
    index_at[longest] = (index_at[longest] + 1) % extent[longest]
    return drawn.at[tuple(index_at)].set(top_value)


def shard_levels(rng, extent, cuts, low, top_value):
    loudness = 1.0
    for axis_at, shards_of in cuts:
        draws = jax.random.uniform(jax.random.fold_in(jax.random.fold_in(rng, 6), axis_at), (shards_of,), jnp.float32, low / len(cuts), top_value / len(cuts))
        loudness = loudness * jnp.repeat(jnp.exp(draws), extent[axis_at] // shards_of).reshape((-1,) + (1,) * (len(extent) - 1 - axis_at))
    return loudness


def scatter_about(stream_key, shape, scale, limit, pieces=(), kind=jnp.bfloat16):
    loudness = shard_levels(stream_key, shape, pieces, -0.22, 0.18) if pieces else 1.0
    entries = jax.random.normal(stream_key, shape, jnp.float32) * scale * loudness
    return jnp.minimum(jnp.maximum(entries, -limit), limit).astype(kind)


def setup_inputs(seed: int = 0) -> dict:
    streams_of = jax.random.split(jax.random.key(seed), 10)
    attention = scatter_about(streams_of[0], (B, D), 1.0, 6.0, ((1, 256),))
    residual = draw_residual(jax.random.fold_in(streams_of[9], 71), 0)
    wo_codes = with_ends(jax.random.randint(streams_of[2], (2, D // GROUP, D), 0, BOOK), jax.random.fold_in(streams_of[2], 1), 0, BOOK - 1).astype(jnp.int32)
    wo_books = scatter_about(streams_of[3], (2, BOOK, GROUP), (2 * D) ** -0.5, 0.03125)
    wo_scale = jnp.clip(jnp.exp(math.log(2.0) - 1.3862944 * jax.random.uniform(streams_of[4], (D,), jnp.float32) ** shard_levels(streams_of[4], (D,), ((0, 32),), -0.2, 0.2)), 0.5, 2.0)
    norm_gain = jnp.clip(1.0 + 0.15 * jax.random.normal(streams_of[5], (D,), jnp.float32), 0.25, 1.75)
    gate_codes = with_ends(jax.random.randint(streams_of[6], (2, D // GROUP, FF), 0, BOOK), jax.random.fold_in(streams_of[6], 1), 0, BOOK - 1).astype(jnp.int32)
    gate_books = scatter_about(streams_of[7], (2, BOOK, GROUP), (2 * D) ** -0.5, 0.03125)
    gate_scale = jnp.clip(jnp.exp(math.log(2.0) - 1.3862944 * jax.random.uniform(streams_of[8], (FF,), jnp.float32) ** shard_levels(streams_of[8], (FF,), ((0, 32),), -0.2, 0.2)), 0.5, 2.0)
    return dict(attention=attention, residual=residual, wo_codes=wo_codes, wo_books=wo_books, wo_scale=wo_scale, norm_gain=norm_gain, gate_codes=gate_codes, gate_books=gate_books, gate_scale=gate_scale)


epsilon = 1e-05

def decompress(codes, books, scale):
    tables = books.astype(jnp.float32)
    first_book = jnp.take(tables[0], codes[0], axis=0)
    second_book = jnp.take(tables[1], codes[1], axis=0)
    summed = first_book + second_book
    groups, outputs = (codes.shape[1], codes.shape[2])
    weight = jnp.transpose(summed, (0, 2, 1)).reshape(groups * GROUP, outputs) * scale[None, :]
    return weight.astype(jnp.bfloat16)

def project(inputs, codes, books, scale):
    groups, outputs = (codes.shape[1], codes.shape[2])
    block_width = math.gcd(outputs, 1024)
    block_count = outputs // block_width
    code_blocks = jnp.transpose(codes.reshape(2, groups, block_count, block_width), (2, 0, 1, 3))
    scale_blocks = scale.reshape(block_count, block_width)

    def one_block(pair):
        weight = decompress(pair[0], books, pair[1])
        return jnp.dot(inputs, weight, preferred_element_type=jnp.float32)
    result = lax.map(one_block, (code_blocks, scale_blocks))
    return jnp.transpose(result, (1, 0, 2)).reshape(inputs.shape[0], outputs)

def reference(attention, residual, wo_codes, wo_books, wo_scale, norm_gain, gate_codes, gate_books, gate_scale):
    projected = project(attention, wo_codes, wo_books, wo_scale)
    hidden = residual.astype(jnp.float32) + projected
    square_mean = lax.optimization_barrier(jnp.mean(hidden * hidden, axis=1, keepdims=True))
    normed = (hidden * lax.rsqrt(square_mean + epsilon) * norm_gain[None, :]).astype(jnp.bfloat16)
    gate_out = project(normed, gate_codes, gate_books, gate_scale).astype(jnp.bfloat16)
    return (hidden.astype(jnp.bfloat16), gate_out)
```

```python
import functools

import jax
import jax.numpy as jnp
from jax import lax
from jax.experimental import pallas as pl
from jax.experimental.pallas import tpu as pltpu
from jax.sharding import PartitionSpec as P

B = 128
BOOK = 256
GROUP = 8
Y = 4
EPS = 1e-05
F32 = jnp.float32
BF16 = jnp.bfloat16
I32 = jnp.int32


def remote(src, dst, send_sem, recv_sem, device):
    return pltpu.make_async_remote_copy(
        src_ref=src,
        dst_ref=dst,
        send_sem=send_sem,
        recv_sem=recv_sem,
        device_id=device,
        device_id_type=pl.DeviceIdType.MESH,
    )


def build_tables(books_ref, tab_ref):
    eye = (
        lax.broadcasted_iota(I32, (8, 8), 0) == lax.broadcasted_iota(I32, (8, 8), 1)
    ).astype(BF16)
    rows = [
        lax.dot_general(eye, books_ref[b], (((1,), (1,)), ((), ())), preferred_element_type=F32)
        for b in range(2)
    ]
    top = jnp.maximum(jnp.abs(rows[0]), jnp.abs(rows[1]))
    top = jnp.max(jnp.max(top, axis=0, keepdims=True), axis=1, keepdims=True)
    scale = jnp.full((1, 1), 2.0**18, F32)
    inverse = jnp.full((1, 1), 2.0**-18, F32)
    for j in range(1, 33):
        fits = top <= 2.0 ** (-5 - j)
        scale = jnp.where(fits, 2.0 ** (18 + j), scale)
        inverse = jnp.where(fits, 2.0 ** (-18 - j), inverse)
    for b in range(2):
        whole = jnp.round(rows[b] * scale).astype(I32)
        for p in range(4):
            word = whole[2 * p : 2 * p + 1] * 65536 + whole[2 * p + 1 : 2 * p + 2]
            for h in range(2):
                tab_ref[b, p, h] = jnp.broadcast_to(word[:, 128 * h : 128 * h + 128], (8, 128))
    return inverse


def pick(table, index):
    return jnp.take_along_axis(table, index, axis=1, mode="promise_in_bounds")


def unpack_rows(codes_ref, tab_ref, weight_ref, block, place):
    tabs = [[[tab_ref[b, p, h] for h in range(2)] for p in range(4)] for b in range(2)]
    for n in range(codes_ref.shape[2] // 128):
        columns = pl.ds(n * 128, 128)
        found = []
        for b in range(2):
            code = codes_ref[b, pl.ds(pl.multiple_of(block * 8, 8), 8), columns]
            low = code & 127
            first = code < 128
            found.append(
                [jnp.where(first, pick(tabs[b][p][0], low), pick(tabs[b][p][1], low)) for p in range(4)]
            )
        for p in range(4):
            word = found[0][p] + found[1][p]
            odd = (word << 16) >> 16
            even = (word - odd) >> 16
            pair = jnp.concatenate([even.astype(F32), odd.astype(F32)], axis=0)
            start = pl.multiple_of(place * 64 + p * 16, 16)
            weight_ref[pl.ds(start, 16), columns] = pair.astype(BF16)


def kernel(
    att_ref, res_ref, wo_codes_hbm, wo_books_ref, wo_scale_ref, gain_ref, gate_codes_hbm,
    gate_books_ref, gate_scale_ref,
    stream_ref, gate_ref,
    wo_codes, gate_codes, wo_tab, gate_tab, xt, w1, acc1, part1, in1, hz, x2, w2, acc2, part2, in2,
    ssz, ssy,
    code_sem, a1s, a1r, a2s, a2r, bs, br, sts, strr, c1s, c1r, c2s, c2r, c3s, c3r, zs, zr, ys, yr, ds, dr,
    *, blocks,
):
    inp, out = lax.axis_index("inp"), lax.axis_index("out")
    n_inp, n_z = lax.axis_size("inp"), lax.axis_size("out") // Y
    z, y = out // Y, out % Y
    rows = B // n_inp

    def at_z(d):
        return {"out": ((z + d) % n_z) * Y + y}

    def at_y(d):
        return {"out": z * Y + (y + d) % Y}

    def at_inp(d):
        return {"inp": (inp + d) % n_inp}

    wo_load = pltpu.make_async_copy(wo_codes_hbm, wo_codes, code_sem.at[0])
    gate_load = pltpu.make_async_copy(gate_codes_hbm, gate_codes, code_sem.at[1])
    wo_load.start()
    gate_load.start()
    barrier = pltpu.get_barrier_semaphore()
    for at, n in ((at_z, n_z), (at_y, Y), (at_inp, n_inp)):
        for d in range(1, n):
            pl.semaphore_signal(
                barrier, inc=1, device_id=at(d), device_id_type=pl.DeviceIdType.MESH
            )

    new = lax.broadcasted_iota(I32, (64, 64), 0)
    old = lax.broadcasted_iota(I32, (64, 64), 1)
    order = (old == 8 * (new % 8) + new // 8).astype(BF16)
    own = lax.dot_general(order, att_ref[...], (((1,), (1,)), ((), ())), preferred_element_type=F32)
    xt[y, z] = own.astype(BF16)
    wo_inverse = build_tables(wo_books_ref, wo_tab)
    gate_inverse = build_tables(gate_books_ref, gate_tab)
    pl.semaphore_wait(barrier, n_z + Y + n_inp - 3)

    a1 = [
        remote(xt.at[y, z], xt.at[y, z], a1s.at[d], a1r.at[z], at_z(d)) for d in range(1, n_z)
    ]
    for copy in a1:
        copy.start()

    def unpack_wo(first, last):
        def step(t, carry):
            for u in range(4):
                block = t * 4 + u
                unpack_rows(wo_codes, wo_tab, w1, block, (block % Y) * n_z + block // Y)
            return carry

        lax.fori_loop(first // 4, last // 4, step, 0)

    def unpack_gate(first, last):
        def step(t, carry):
            for u in range(2):
                block = t * 2 + u
                unpack_rows(gate_codes, gate_tab, w2, block, block)
            return carry

        lax.fori_loop(first // 2, last // 2, step, 0)

    wo_load.wait()
    unpack_wo(0, 16)
    for d in range(1, n_z):
        source = (z + d) % n_z
        remote(xt.at[y, z], xt.at[y, source], a1s.at[0], a1r.at[source], at_z(d)).wait_recv()
    a2 = [remote(xt.at[y], xt.at[y], a2s.at[d], a2r.at[y], at_y(d)) for d in range(1, Y)]
    for copy in a2:
        copy.start()
    unpack_wo(16, 32)
    gate_load.wait()
    unpack_gate(0, 8)

    def project(source, first):
        lhs = xt[source].reshape(n_z * 64, B)
        start = pl.multiple_of(source * (n_z * 64), n_z * 64)
        product = lax.dot_general(
            lhs, w1[pl.ds(start, n_z * 64), :], (((0,), (0,)), ((), ())), preferred_element_type=F32
        )
        if first:
            acc1[...] = product
        else:
            acc1[...] += product

    project(y, True)
    for d in (1, 3, 2):
        source = (y + d) % Y
        remote(xt.at[y], xt.at[source], a2s.at[0], a2r.at[source], at_y(d)).wait_recv()
        project(source, False)
    part1[...] = acc1[...].astype(BF16).reshape(part1.shape)
    b = [
        remote(part1.at[(inp + d) % n_inp], in1.at[inp], bs.at[d], br.at[inp], at_inp(d))
        for d in range(1, n_inp)
    ]
    for copy in b:
        copy.start()
    unpack_gate(8, 14)

    own_rows = pl.ds(pl.multiple_of(inp * rows, rows), rows)
    total = acc1[own_rows, :]
    for d in range(1, n_inp):
        source = (inp + d) % n_inp
        remote(part1.at[inp], in1.at[source], bs.at[0], br.at[source], at_inp(d)).wait_recv()
        total = total + in1[source].astype(F32)
    hidden = res_ref[own_rows, :].astype(F32) + total * (wo_scale_ref[...] * wo_inverse)
    gained = (hidden * gain_ref[out]).astype(BF16)
    new = lax.broadcasted_iota(I32, (128, 128), 1)
    old = lax.broadcasted_iota(I32, (128, 128), 0)
    order = (old == 64 * (new // 64) + 8 * (new % 8) + (new % 64) // 8).astype(BF16)
    for n in range(gained.shape[1] // 128):
        columns = pl.ds(n * 128, 128)
        hz[z, :, columns] = jnp.dot(
            gained[:, n * 128 : n * 128 + 128], order, preferred_element_type=F32
        ).astype(BF16)
    c1 = [remote(hz.at[z], hz.at[z], c1s.at[d], c1r.at[z], at_z(d)) for d in range(1, n_z)]
    for copy in c1:
        copy.start()

    row = lax.broadcasted_iota(I32, (rows, 128), 0)
    lane = lax.broadcasted_iota(I32, (rows, 128), 1)
    squares = jnp.sum(hidden * hidden, axis=1, keepdims=True)
    ssz[z] = jnp.sum(jnp.where(row == lane, squares, 0.0), axis=0, keepdims=True)
    z_sums = [remote(ssz.at[z], ssz.at[z], zs.at[d], zr.at[z], at_z(d)) for d in range(1, n_z)]
    for copy in z_sums:
        copy.start()
    stream_ref[own_rows, :] = hidden.astype(BF16)
    stream_copies = [
        remote(stream_ref.at[own_rows], stream_ref.at[own_rows], sts.at[d], strr.at[inp], at_inp(d))
        for d in range(1, n_inp)
    ]
    for copy in stream_copies:
        copy.start()
    unpack_gate(14, 20)

    for d in range(n_inp):
        target = (inp + d) % n_inp

        @pl.when(target != z)
        def _():
            remote(hz.at[z], hz.at[target], c1s.at[0], c1r.at[target], at_z(1)).wait_recv()

        if d == 0:
            x2[y, own_rows, :] = hz[target]
        else:
            remote(hz.at[target], x2.at[y, own_rows], c2s.at[d], c2r.at[inp], at_inp(d)).start()
    unpack_gate(20, 26)
    for d in range(1, n_z):
        source = (z + d) % n_z
        remote(ssz.at[z], ssz.at[source], zs.at[0], zr.at[source], at_z(d)).wait_recv()
    ssy[y] = jnp.sum(ssz[...], axis=0)
    y_sums = [remote(ssy.at[y], ssy.at[y], ys.at[d], yr.at[y], at_y(d)) for d in range(1, Y)]
    for copy in y_sums:
        copy.start()
    for d in range(1, n_inp):
        source = (inp + d) % n_inp
        source_rows = pl.ds(pl.multiple_of(source * rows, rows), rows)
        remote(
            hz.at[z], x2.at[y, source_rows], c2s.at[0], c2r.at[source], at_inp(d)
        ).wait_recv()
    c3 = [remote(x2.at[y], x2.at[y], c3s.at[d], c3r.at[y], at_y(d)) for d in range(1, Y)]
    for copy in c3:
        copy.start()
    unpack_gate(26, 32)

    depth = x2.shape[2]

    def gate_rows(source):
        return pl.ds(pl.multiple_of(source * depth, depth), depth)

    for d in (0, 1, 3):
        source = (y + d) % Y
        if d:
            remote(x2.at[y], x2.at[source], c3s.at[0], c3r.at[source], at_y(d)).wait_recv()
        for start, width in blocks:
            columns = pl.ds(start, width)
            product = jnp.dot(
                x2[source], w2[gate_rows(source), columns], preferred_element_type=F32
            )
            if d:
                acc2[:, columns] += product
            else:
                acc2[:, columns] = product
    source = (y + 2) % Y
    remote(x2.at[y], x2.at[source], c3s.at[0], c3r.at[source], at_y(2)).wait_recv()
    for k, (start, width) in enumerate(blocks):
        columns = pl.ds(start, width)
        product = acc2[:, columns] + jnp.dot(
            x2[source], w2[gate_rows(source), columns], preferred_element_type=F32
        )
        acc2[:, columns] = product
        part2[:, :, columns] = product.astype(BF16).reshape(n_inp, rows, width)
        for d in range(1, n_inp):
            remote(
                part2.at[(inp + d) % n_inp, :, columns],
                in2.at[inp, :, columns],
                ds.at[k, d],
                dr.at[k, inp],
                at_inp(d),
            ).start()

    for d in range(1, Y):
        source = (y + d) % Y
        remote(ssy.at[y], ssy.at[source], ys.at[0], yr.at[source], at_y(d)).wait_recv()
    mean = jnp.sum(ssy[...], axis=0) * (1.0 / (depth * Y * n_z))
    mean = jnp.sum(jnp.where(row == lane, mean, 0.0), axis=1, keepdims=True)
    factor = lax.rsqrt(mean + EPS) * gate_inverse

    for k, (start, width) in enumerate(blocks):
        columns = pl.ds(start, width)
        total = acc2[own_rows, columns]
        for d in range(1, n_inp):
            source = (inp + d) % n_inp
            remote(
                part2.at[inp, :, columns],
                in2.at[source, :, columns],
                ds.at[k, 0],
                dr.at[k, source],
                at_inp(d),
            ).wait_recv()
            total = total + in2[source, :, columns].astype(F32)
        gate_ref[:, columns] = (total * (factor * gate_scale_ref[:, columns])).astype(BF16)

    for d in range(1, n_inp):
        source = (inp + d) % n_inp
        source_rows = pl.ds(pl.multiple_of(source * rows, rows), rows)
        remote(
            stream_ref.at[own_rows], stream_ref.at[source_rows], sts.at[0], strr.at[source], at_inp(d)
        ).wait_recv()
    for copy in a1 + a2 + b + c1 + z_sums + stream_copies + y_sums + c3:
        copy.wait_send()
    for d in range(1, n_inp):
        remote(hz.at[z], x2.at[y, own_rows], c2s.at[d], c2r.at[inp], at_inp(d)).wait_send()
        for k, (start, width) in enumerate(blocks):
            columns = pl.ds(start, width)
            remote(
                part2.at[inp, :, columns],
                in2.at[inp, :, columns],
                ds.at[k, d],
                dr.at[k, inp],
                at_inp(d),
            ).wait_send()


def per_device(
    attention, residual, wo_codes, wo_books, wo_scale, norm_gain, gate_codes, gate_books, gate_scale
):
    n_inp, n_out = lax.axis_size("inp"), lax.axis_size("out")
    n_z = n_out // Y
    rows = B // n_inp
    width, gate_width = wo_codes.shape[2], gate_codes.shape[2]
    depth = wo_codes.shape[1] * GROUP
    blocks = ((0, 384), (384, 384), (768, 384), (1152, 512))
    vmem = pl.BlockSpec(memory_space=pltpu.VMEM)
    hbm = pl.BlockSpec(memory_space=pl.ANY)
    dma = pltpu.SemaphoreType.DMA
    return pl.pallas_call(
        functools.partial(kernel, blocks=blocks),
        out_shape=(
            jax.ShapeDtypeStruct((B, width), BF16),
            jax.ShapeDtypeStruct((rows, gate_width), BF16),
        ),
        in_specs=[vmem, vmem, hbm, vmem, vmem, vmem, hbm, vmem, vmem],
        out_specs=(vmem, vmem),
        scratch_shapes=[
            pltpu.VMEM(wo_codes.shape, I32),
            pltpu.VMEM(gate_codes.shape, I32),
            pltpu.VMEM((2, 4, 2, 8, 128), I32),
            pltpu.VMEM((2, 4, 2, 8, 128), I32),
            pltpu.VMEM((Y, n_z, 64, B), BF16),
            pltpu.VMEM((depth, width), BF16),
            pltpu.VMEM((B, width), F32),
            pltpu.VMEM((n_inp, rows, width), BF16),
            pltpu.VMEM((n_inp, rows, width), BF16),
            pltpu.VMEM((n_z, rows, width), BF16),
            pltpu.VMEM((Y, B, width), BF16),
            pltpu.VMEM((depth, gate_width), BF16),
            pltpu.VMEM((B, gate_width), F32),
            pltpu.VMEM((n_inp, rows, gate_width), BF16),
            pltpu.VMEM((n_inp, rows, gate_width), BF16),
            pltpu.VMEM((n_z, 1, 128), F32),
            pltpu.VMEM((Y, 1, 128), F32),
            dma((2,)),
            dma((n_z,)), dma((n_z,)),
            dma((Y,)), dma((Y,)),
            dma((n_inp,)), dma((n_inp,)),
            dma((n_inp,)), dma((n_inp,)),
            dma((n_z,)), dma((n_z,)),
            dma((n_inp,)), dma((n_inp,)),
            dma((Y,)), dma((Y,)),
            dma((n_z,)), dma((n_z,)),
            dma((Y,)), dma((Y,)),
            dma((len(blocks), n_inp)), dma((len(blocks), n_inp)),
        ],
        compiler_params=pltpu.CompilerParams(
            collective_id=0, has_side_effects=True, vmem_limit_bytes=40 << 20
        ),
        name="step",
    )(
        attention, residual, wo_codes, wo_books, wo_scale[None, :], norm_gain.reshape(n_out, 1, width),
        gate_codes, gate_books, gate_scale[None, :],
    )


def solution(mesh):
    placed = (
        P(None, ("inp", "out")),
        P(None, "out"),
        P(None, "inp", "out"),
        P(),
        P("out"),
        P(),
        P(None, "inp", "out"),
        P(),
        P("out"),
    )
    return jax.shard_map(
        per_device,
        mesh=mesh,
        in_specs=placed,
        out_specs=(P(None, "out"), P("inp", "out")),
        check_vma=False,
    )
```

```python
import functools

import jax
import jax.numpy as jnp
from jax import lax
from jax.experimental import pallas as pl
from jax.experimental.pallas import tpu as pltpu
from jax.sharding import PartitionSpec as P

B = 128
BOOK = 256
GROUP = 8
Y = 4
EPS = 1e-05
F32 = jnp.float32
BF16 = jnp.bfloat16
I32 = jnp.int32


def remote(src, dst, send_sem, recv_sem, device):
    return pltpu.make_async_remote_copy(
        src_ref=src,
        dst_ref=dst,
        send_sem=send_sem,
        recv_sem=recv_sem,
        device_id=device,
        device_id_type=pl.DeviceIdType.MESH,
    )


def build_tables(books_ref, tab_ref):
    rows = [books_ref[b].astype(F32) for b in range(2)]
    top = jnp.maximum(jnp.abs(rows[0]), jnp.abs(rows[1]))
    top = jnp.max(jnp.max(top, axis=0, keepdims=True), axis=1, keepdims=True)
    scale = jnp.full((1, 1), 2.0**18, F32)
    inverse = jnp.full((1, 1), 2.0**-18, F32)
    for j in range(1, 33):
        fits = top <= 2.0 ** (-5 - j)
        scale = jnp.where(fits, 2.0 ** (18 + j), scale)
        inverse = jnp.where(fits, 2.0 ** (-18 - j), inverse)
    for b in range(2):
        whole = jnp.round(rows[b] * scale).astype(I32)
        for p in range(4):
            word = whole[2 * p : 2 * p + 1] * 65536 + whole[2 * p + 1 : 2 * p + 2]
            for h in range(2):
                tab_ref[b, p, h] = jnp.broadcast_to(word[:, 128 * h : 128 * h + 128], (8, 128))
    return inverse


def pick(table, index):
    return jnp.take_along_axis(table, index, axis=1, mode="promise_in_bounds")


def unpack_rows(codes_ref, tab_ref, scale_ref, weight_ref, block, place):
    tabs = [[[tab_ref[b, p, h] for h in range(2)] for p in range(4)] for b in range(2)]
    for n in range(codes_ref.shape[2] // 128):
        columns = pl.ds(n * 128, 128)
        scale = jnp.broadcast_to(scale_ref[:, columns], (16, 128))
        found = []
        for b in range(2):
            code = codes_ref[b, pl.ds(pl.multiple_of(block * 8, 8), 8), columns]
            low = code & 127
            first = code < 128
            found.append(
                [jnp.where(first, pick(tabs[b][p][0], low), pick(tabs[b][p][1], low)) for p in range(4)]
            )
        for p in range(4):
            word = found[0][p] + found[1][p]
            odd = (word << 16) >> 16
            even = (word - odd) >> 16
            pair = jnp.concatenate([even.astype(F32), odd.astype(F32)], axis=0) * scale
            start = pl.multiple_of(place * 64 + p * 16, 16)
            weight_ref[pl.ds(start, 16), columns] = pair.astype(BF16)


def offset(t, n):
    return (t % 2) * ((t + 1) // 2) + (1 - t % 2) * ((n - t // 2) % n)


def kernel(
    att_hbm, res_hbm, wo_codes_hbm, wo_books_hbm, wo_scale_hbm, gain_hbm, gate_codes_hbm, gate_books_hbm,
    gate_scale_hbm,
    stream_ref, gate_ref,
    att, res, wo_codes, wo_books, wo_scale, gain, gate_codes, gate_books, gate_scale_flat,
    gate_scale, wo_tab, gate_tab, xt, w1, acc1, part1, in1, hz, x2, w2, acc2, part2, pair2, send2, in2, ssz, ssy,
    load_sem, a1s, a1r, a2s, a2r, bs, br, sts, strr, c1s, c1r, c2s, c2r, own_sem, zs, zr, ys, yr,
    d1s, d1r, d2s, d2r,
    *, blocks, early, middle, late,
):
    inp, out = lax.axis_index("inp"), lax.axis_index("out")
    n_inp, n_z = lax.axis_size("inp"), lax.axis_size("out") // Y
    n_x = n_inp // 2
    z, y, x, core = out // Y, out % Y, inp // 2, inp % 2
    rows = B // n_inp
    own_rows = pl.ds(pl.multiple_of(inp * rows, rows), rows)

    def at_z(d):
        return {"out": ((z + d) % n_z) * Y + y}

    def at_y(d):
        return {"out": z * Y + (y + d) % Y}

    def at_inp(d):
        return {"inp": (inp + d) % n_inp}

    loads = [
        pltpu.make_async_copy(src, dst, load_sem.at[k])
        for k, (src, dst) in enumerate(
            (
                (att_hbm, att),
                (wo_books_hbm, wo_books),
                (wo_scale_hbm, wo_scale),
                (wo_codes_hbm, wo_codes),
                (gate_books_hbm, gate_books),
                (gate_scale_hbm, gate_scale_flat),
                (gate_codes_hbm, gate_codes),
                (res_hbm.at[own_rows], res),
                (gain_hbm.at[out], gain),
            )
        )
    ]
    loads[0].start()
    barrier = pltpu.get_barrier_semaphore()
    for at, n in ((at_z, n_z), (at_y, Y), (at_inp, n_inp)):
        for d in range(1, n):
            pl.semaphore_signal(
                barrier, inc=1, device_id=at(d), device_id_type=pl.DeviceIdType.MESH
            )
    for load in loads[1:]:
        load.start()

    new = lax.broadcasted_iota(I32, (64, 64), 0)
    old = lax.broadcasted_iota(I32, (64, 64), 1)
    order = (old == 8 * (new % 8) + new // 8).astype(BF16)
    loads[0].wait()
    xt[y, z] = jnp.dot(order, att[...], preferred_element_type=F32).astype(BF16)
    pl.semaphore_wait(barrier, n_z + Y + n_inp - 3)

    def a1(t):
        d = offset(t, n_z)
        return remote(xt.at[y, z], xt.at[y, z], a1s.at[t], a1r.at[z], at_z(d))

    def a2(t, d):
        tile = (z + offset(t, n_z)) % n_z
        return remote(xt.at[y, tile], xt.at[y, tile], a2s.at[t, d], a2r.at[y, tile], at_y(d))

    for t in range(1, n_z):
        a1(t).start()
    for d in (1, 3, 2):
        a2(0, d).start()

    for load in loads[1:6]:
        load.wait()
    wo_inverse = build_tables(wo_books, wo_tab)
    wo_scale[...] = wo_scale[...] * wo_inverse
    gate_inverse = build_tables(gate_books, gate_tab)
    gate_scale[...] = gate_scale_flat[...][None, :] * gate_inverse

    def unpack_wo(t):
        for u in range(Y):
            block = t * Y + u
            unpack_rows(wo_codes, wo_tab, wo_scale, w1, block, u * n_z + t)

    def unpack_gate(first, last):
        def step(t, carry):
            for u in range(2):
                block = t * 2 + u
                unpack_rows(gate_codes, gate_tab, gate_scale, w2, block, block)
            return carry

        lax.fori_loop(first // 2, last // 2, step, 0)

    unpack_wo(0)

    def relay_features(t, carry):
        tile = (z + offset(t, n_z)) % n_z
        remote(xt.at[y, z], xt.at[y, tile], a1s.at[0], a1r.at[tile], at_z(1)).wait_recv()
        for d in (1, 3, 2):
            a2(t, d).start()
        unpack_wo(t)
        return carry

    lax.fori_loop(1, n_z, relay_features, 0)
    loads[6].wait()
    unpack_gate(0, early)

    def project(source, first):
        lhs = xt[source].reshape(n_z * 64, B)
        start = pl.multiple_of(source * (n_z * 64), n_z * 64)
        product = lax.dot_general(
            lhs, w1[pl.ds(start, n_z * 64), :], (((0,), (0,)), ((), ())), preferred_element_type=F32
        )
        if first:
            acc1[...] = product
        else:
            acc1[...] += product

    project(y, True)
    for d in (1, 3, 2):
        source = (y + d) % Y
        for t in range(n_z):
            remote(xt.at[y, t], xt.at[source, t], a2s.at[0, 0], a2r.at[source, t], at_y(d)).wait_recv()
        project(source, False)
    part1[...] = acc1[...].astype(BF16).reshape(part1.shape)

    def b(d):
        return remote(part1.at[(inp + d) % n_inp], in1.at[inp], bs.at[d], br.at[inp], at_inp(d))

    for d in range(1, n_inp):
        b(d).start()
    loads[7].wait()
    loads[8].wait()
    unpack_gate(early, early + middle)

    total = acc1[own_rows, :]
    for d in range(1, n_inp):
        source = (inp + d) % n_inp
        remote(part1.at[inp], in1.at[source], bs.at[0], br.at[source], at_inp(d)).wait_recv()
        total = total + in1[source].astype(F32)
    hidden = res[...].astype(F32) + total
    gained = (hidden * gain[...]).astype(BF16)
    new = lax.broadcasted_iota(I32, (128, 128), 1)
    old = lax.broadcasted_iota(I32, (128, 128), 0)
    order = (old == 64 * (new // 64) + 8 * (new % 8) + (new % 64) // 8).astype(BF16)
    for n in range(gained.shape[1] // 128):
        hz[z, :, pl.ds(n * 128, 128)] = jnp.dot(
            gained[:, n * 128 : n * 128 + 128], order, preferred_element_type=F32
        ).astype(BF16)

    def c1(t):
        return remote(hz.at[z], hz.at[z], c1s.at[t], c1r.at[z], at_z(offset(t, n_z)))

    for t in range(1, n_z):
        c1(t).start()

    def c2(t, d):
        tile = (z + offset(t, n_z)) % n_z
        target = {"inp": tile, "out": z * Y + (y + d) % Y}
        return remote(hz.at[tile], x2.at[y, own_rows], c2s.at[t, d], c2r.at[y, inp], target)

    own_copy = pltpu.make_async_copy(hz.at[inp], x2.at[y, own_rows], own_sem)

    def spread(t):
        tile = (z + offset(t, n_z)) % n_z
        for d in (2, 1, 3):
            c2(t, d).start()

        @pl.when(tile != inp)
        def _():
            c2(t, 0).start()

        @pl.when(tile == inp)
        def _():
            own_copy.start()

    spread(0)
    row = lax.broadcasted_iota(I32, (rows, 128), 0)
    lane = lax.broadcasted_iota(I32, (rows, 128), 1)
    squares = jnp.sum(hidden * hidden, axis=1, keepdims=True)
    ssz[z] = jnp.sum(jnp.where(row == lane, squares, 0.0), axis=0, keepdims=True)
    stream_ref[own_rows, :] = hidden.astype(BF16)

    def z_sum(d):
        return remote(ssz.at[z], ssz.at[z], zs.at[d], zr.at[z], at_z(d))

    def y_sum(d):
        return remote(ssy.at[y], ssy.at[y], ys.at[d], yr.at[y], at_y(d))

    def stream(d):
        return remote(
            stream_ref.at[own_rows], stream_ref.at[own_rows], sts.at[d], strr.at[inp], at_inp(d)
        )

    for d in range(1, n_z):
        z_sum(d).start()

    def relay_tiles(t, carry):
        tile = (z + offset(t, n_z)) % n_z
        remote(hz.at[z], hz.at[tile], c1s.at[0], c1r.at[tile], at_z(1)).wait_recv()
        spread(t)

        @pl.when(t <= late // 2)
        def _():
            for u in range(2):
                block = early + middle + (t - 1) * 2 + u
                unpack_rows(gate_codes, gate_tab, gate_scale, w2, block, block)

        return carry

    lax.fori_loop(1, n_z, relay_tiles, 0)
    for d in range(1, n_z):
        source = (z + d) % n_z
        remote(ssz.at[z], ssz.at[source], zs.at[0], zr.at[source], at_z(d)).wait_recv()
    ssy[y] = jnp.sum(ssz[...], axis=0)
    for d in range(1, Y):
        y_sum(d).start()
    for d in range(1, n_inp):
        stream(d).start()

    depth = x2.shape[2]

    def gate_rows(source):
        return pl.ds(pl.multiple_of(source * depth, depth), depth)

    def arrived(d):
        source = (y + d) % Y
        for e in range(n_inp):
            sender = (inp + e) % n_inp
            if d == 0 and e == 0:
                own_copy.wait()
            else:
                there = x2.at[source, pl.ds(pl.multiple_of(sender * rows, rows), rows)]
                remote(hz.at[z], there, c2s.at[0, 0], c2r.at[source, sender], at_y(1)).wait_recv()
        return source

    for d in (0, 1, 3):
        source = arrived(d)
        for start, width in blocks:
            columns = pl.ds(start, width)
            product = jnp.dot(
                x2[source], w2[gate_rows(source), columns], preferred_element_type=F32
            ).reshape(n_x, 2, rows, width)
            if d:
                acc2[:, :, :, columns] += product
            else:
                acc2[:, :, :, columns] = product

    def d1(k):
        columns = pl.ds(*blocks[k])
        return remote(
            part2.at[:, :, columns], pair2.at[:, :, columns], d1s.at[k], d1r.at[k],
            {"inp": 2 * x + 1 - core},
        )

    def d2(k, d):
        columns = pl.ds(*blocks[k])
        return remote(
            send2.at[(x + d) % n_x, :, columns], in2.at[x, :, columns], d2s.at[k, d], d2r.at[k, x],
            {"inp": ((x + d) % n_x) * 2 + core},
        )

    source = arrived(2)
    for k, (start, width) in enumerate(blocks):
        columns = pl.ds(start, width)
        acc2[:, :, :, columns] += jnp.dot(
            x2[source], w2[gate_rows(source), columns], preferred_element_type=F32
        ).reshape(n_x, 2, rows, width)
        part2[:, :, columns] = acc2[:, 1 - core, :, columns].astype(BF16)
        d1(k).start()
    for k, (start, width) in enumerate(blocks):
        columns = pl.ds(start, width)
        d1(k).wait_recv()
        both = acc2[:, core, :, columns] + pair2[:, :, columns].astype(F32)
        acc2[:, core, :, columns] = both
        send2[:, :, columns] = both.astype(BF16)
        for d in (2, 1, 3):
            d2(k, d).start()

    for d in range(1, Y):
        source = (y + d) % Y
        remote(ssy.at[y], ssy.at[source], ys.at[0], yr.at[source], at_y(d)).wait_recv()
    mean = jnp.sum(ssy[...], axis=0) * (1.0 / (depth * Y * n_z))
    mean = jnp.sum(jnp.where(row == lane, mean, 0.0), axis=1, keepdims=True)
    factor = lax.rsqrt(mean + EPS)

    for d in range(1, n_inp):
        source = (inp + d) % n_inp
        source_rows = pl.ds(pl.multiple_of(source * rows, rows), rows)
        remote(
            stream_ref.at[own_rows], stream_ref.at[source_rows], sts.at[0], strr.at[source], at_inp(d)
        ).wait_recv()
        b(d).wait_send()
        stream(d).wait_send()
    for d in range(1, n_z):
        z_sum(d).wait_send()
    for d in range(1, Y):
        y_sum(d).wait_send()

    def sent(t, carry):
        @pl.when(t > 0)
        def _():
            a1(t).wait_send()
            c1(t).wait_send()

        for d in (1, 3, 2):
            a2(t, d).wait_send()
            c2(t, d).wait_send()

        @pl.when((z + offset(t, n_z)) % n_z != inp)
        def _():
            c2(t, 0).wait_send()

        return carry

    lax.fori_loop(0, n_z, sent, 0)

    for k, (start, width) in enumerate(blocks):
        columns = pl.ds(start, width)
        total = acc2[x, core, :, columns]
        for d in (1, 3, 2):
            source = (x + d) % n_x
            remote(
                send2.at[x, :, columns], in2.at[source, :, columns], d2s.at[k, 0], d2r.at[k, source],
                {"inp": source * 2 + core},
            ).wait_recv()
            total = total + in2[source, :, columns].astype(F32)
        gate_ref[:, columns] = (total * factor).astype(BF16)
        d1(k).wait_send()
        for d in range(1, n_x):
            d2(k, d).wait_send()


def per_device(
    attention, residual, wo_codes, wo_books, wo_scale, norm_gain, gate_codes, gate_books, gate_scale
):
    n_inp, n_out = lax.axis_size("inp"), lax.axis_size("out")
    n_z, n_x = n_out // Y, n_inp // 2
    rows = B // n_inp
    width, gate_width = wo_codes.shape[2], gate_codes.shape[2]
    depth = wo_codes.shape[1] * GROUP
    blocks = ((0, 896), (896, 768))
    vmem = pl.BlockSpec(memory_space=pltpu.VMEM)
    hbm = pl.BlockSpec(memory_space=pltpu.HBM)
    dma = pltpu.SemaphoreType.DMA
    args = (
        attention.T, residual, wo_codes, jnp.swapaxes(wo_books, 1, 2), wo_scale[None, :],
        norm_gain.reshape(n_out, 1, width), gate_codes, jnp.swapaxes(gate_books, 1, 2), gate_scale,
    )
    held = [pltpu.VMEM(a.shape, a.dtype) for a in args]
    held[1] = pltpu.VMEM((rows, width), BF16)
    held[5] = pltpu.VMEM((1, width), F32)
    return pl.pallas_call(
        functools.partial(kernel, blocks=blocks, early=16, middle=6, late=10),
        out_shape=(
            jax.ShapeDtypeStruct((B, width), BF16),
            jax.ShapeDtypeStruct((rows, gate_width), BF16),
        ),
        in_specs=[hbm] * 9,
        out_specs=(vmem, vmem),
        scratch_shapes=[
            *held,
            pltpu.VMEM((1, gate_width), F32),
            pltpu.VMEM((2, 4, 2, 8, 128), I32),
            pltpu.VMEM((2, 4, 2, 8, 128), I32),
            pltpu.VMEM((Y, n_z, 64, B), BF16),
            pltpu.VMEM((depth, width), BF16),
            pltpu.VMEM((B, width), F32),
            pltpu.VMEM((n_inp, rows, width), BF16),
            pltpu.VMEM((n_inp, rows, width), BF16),
            pltpu.VMEM((n_z, rows, width), BF16),
            pltpu.VMEM((Y, B, width), BF16),
            pltpu.VMEM((depth, gate_width), BF16),
            pltpu.VMEM((n_x, 2, rows, gate_width), F32),
            pltpu.VMEM((n_x, rows, gate_width), BF16),
            pltpu.VMEM((n_x, rows, gate_width), BF16),
            pltpu.VMEM((n_x, rows, gate_width), BF16),
            pltpu.VMEM((n_x, rows, gate_width), BF16),
            pltpu.VMEM((n_z, 1, 128), F32),
            pltpu.VMEM((Y, 1, 128), F32),
            dma((9,)),
            dma((n_z,)), dma((n_z,)),
            dma((n_z, Y)), dma((Y, n_z)),
            dma((n_inp,)), dma((n_inp,)),
            dma((n_inp,)), dma((n_inp,)),
            dma((n_z,)), dma((n_z,)),
            dma((n_z, Y)), dma((Y, n_inp)), dma,
            dma((n_z,)), dma((n_z,)),
            dma((Y,)), dma((Y,)),
            dma((len(blocks),)), dma((len(blocks),)),
            dma((len(blocks), n_x)), dma((len(blocks), n_x)),
        ],
        compiler_params=pltpu.CompilerParams(
            collective_id=0, has_side_effects=True, vmem_limit_bytes=63 << 20
        ),
        name="step",
    )(*args)


def solution(mesh):
    placed = (
        P(None, ("inp", "out")),
        P(None, "out"),
        P(None, "inp", "out"),
        P(),
        P("out"),
        P(),
        P(None, "inp", "out"),
        P(),
        P("out"),
    )
    return jax.shard_map(
        per_device,
        mesh=mesh,
        in_specs=placed,
        out_specs=(P(None, "out"), P("inp", "out")),
        check_vma=False,
    )
```

```python
import functools

import jax
import jax.numpy as jnp
from jax import lax
from jax.experimental import pallas as pl
from jax.experimental.pallas import tpu as pltpu
from jax.sharding import PartitionSpec as P

B = 128
BOOK = 256
GROUP = 8
Y = 4
EPS = 1e-05
F32 = jnp.float32
BF16 = jnp.bfloat16
I32 = jnp.int32


def remote(src, dst, send_sem, recv_sem, device):
    return pltpu.make_async_remote_copy(
        src_ref=src,
        dst_ref=dst,
        send_sem=send_sem,
        recv_sem=recv_sem,
        device_id=device,
        device_id_type=pl.DeviceIdType.MESH,
    )


def build_tables(books_ref, tab_ref):
    rows = [books_ref[b].astype(F32) for b in range(2)]
    top = jnp.maximum(jnp.abs(rows[0]), jnp.abs(rows[1]))
    top = jnp.max(jnp.max(top, axis=0, keepdims=True), axis=1, keepdims=True)
    scale = jnp.full((1, 1), 2.0**18, F32)
    inverse = jnp.full((1, 1), 2.0**-18, F32)
    for j in range(1, 33):
        fits = top <= 2.0 ** (-5 - j)
        scale = jnp.where(fits, 2.0 ** (18 + j), scale)
        inverse = jnp.where(fits, 2.0 ** (-18 - j), inverse)
    for b in range(2):
        whole = jnp.round(rows[b] * scale).astype(I32)
        for p in range(4):
            word = whole[2 * p : 2 * p + 1] * 65536 + whole[2 * p + 1 : 2 * p + 2]
            for h in range(2):
                tab_ref[b, p, h] = jnp.broadcast_to(word[:, 128 * h : 128 * h + 128], (8, 128))
    return inverse


def pick(table, index):
    return jnp.take_along_axis(table, index, axis=1, mode="promise_in_bounds")


def unpack_rows(codes_ref, tab_ref, scale_ref, weight_ref, block, place):
    tabs = [[[tab_ref[b, p, h] for h in range(2)] for p in range(4)] for b in range(2)]
    for n in range(codes_ref.shape[2] // 128):
        columns = pl.ds(n * 128, 128)
        scale = jnp.broadcast_to(scale_ref[:, columns], (16, 128))
        found = []
        for b in range(2):
            code = codes_ref[b, pl.ds(pl.multiple_of(block * 8, 8), 8), columns]
            low = code & 127
            first = code < 128
            found.append(
                [jnp.where(first, pick(tabs[b][p][0], low), pick(tabs[b][p][1], low)) for p in range(4)]
            )
        for p in range(4):
            word = found[0][p] + found[1][p]
            odd = (word << 16) >> 16
            even = (word - odd) >> 16
            pair = jnp.concatenate([even.astype(F32), odd.astype(F32)], axis=0) * scale
            start = pl.multiple_of(place * 64 + p * 16, 16)
            weight_ref[pl.ds(start, 16), columns] = pair.astype(BF16)


def offset(t, n):
    return (t % 2) * ((t + 1) // 2) + (1 - t % 2) * ((n - t // 2) % n)


def kernel(
    att_hbm, res_hbm, wo_codes_hbm, wo_books_hbm, wo_scale_hbm, gain_hbm, gate_codes_hbm, gate_books_hbm,
    gate_scale_hbm,
    stream_ref, gate_ref,
    att, res, wo_codes, wo_books, wo_scale, gain, gate_codes, gate_books, gate_scale_flat,
    gate_scale, wo_tab, gate_tab, xt, w1, acc1, part1, in1, x2, w2, acc2, part2, pair2, send2, in2, squares_in, squares_y, squares_all, res_in,
    load_sem, ready, a1s, a1r, a2s, a2r, rs, rr, bs, br, sts, strr, c1s, c1r, c2s, c2r, qs, qr, ys, yr, zs, zr,
    d1s, d1r, d2s, d2r,
    *, blocks, early, middle, late,
):
    inp, out = lax.axis_index("inp"), lax.axis_index("out")
    n_inp, n_z = lax.axis_size("inp"), lax.axis_size("out") // Y
    n_x = n_inp // 2
    z, y, x, core = out // Y, out % Y, inp // 2, inp % 2
    rows = B // n_inp
    diagonal = inp == z

    def row_slice(r):
        return pl.ds(pl.multiple_of(r * rows, rows), rows)

    def at_z(d):
        return {"out": ((z + d) % n_z) * Y + y}

    def at_y(d):
        return {"out": z * Y + (y + d) % Y}

    def at_inp(d):
        return {"inp": (inp + d) % n_inp}

    loads = [
        pltpu.make_async_copy(src, dst, load_sem.at[k])
        for k, (src, dst) in enumerate(
            (
                (att_hbm, att),
                (wo_books_hbm, wo_books),
                (wo_scale_hbm, wo_scale),
                (wo_codes_hbm, wo_codes),
                (gate_books_hbm, gate_books),
                (gate_scale_hbm, gate_scale_flat),
                (gate_codes_hbm, gate_codes),
                (res_hbm.at[row_slice(inp)], res),
                (gain_hbm.at[inp * Y + y], gain),
            )
        )
    ]
    loads[0].start()
    barrier = pltpu.get_barrier_semaphore()
    for at, n in ((at_z, n_z), (at_y, Y), (at_inp, n_inp)):
        for d in range(1, n):
            pl.semaphore_signal(
                barrier, inc=1, device_id=at(d), device_id_type=pl.DeviceIdType.MESH
            )
    for load in loads[1:]:
        load.start()

    new = lax.broadcasted_iota(I32, (64, 64), 0)
    old = lax.broadcasted_iota(I32, (64, 64), 1)
    order = (old == 8 * (new % 8) + new // 8).astype(BF16)
    loads[0].wait()
    xt[y, z] = jnp.dot(order, att[...], preferred_element_type=F32).astype(BF16)
    pl.semaphore_wait(barrier, n_z + Y + n_inp - 3)

    def a1(t):
        d = offset(t, n_z)
        return remote(xt.at[y, z], xt.at[y, z], a1s.at[t], a1r.at[z], at_z(d))

    def a2(t, d):
        tile = (z + offset(t, n_z)) % n_z
        return remote(xt.at[y, tile], xt.at[y, tile], a2s.at[t, d], a2r.at[y, tile], at_y(d))

    for t in range(1, n_z):
        a1(t).start()
    for d in (1, 3, 2):
        a2(0, d).start()

    @pl.when(diagonal)
    def _():
        for d in range(1, n_inp):
            pl.semaphore_signal(
                ready, inc=1, device_id=at_inp(d), device_id_type=pl.DeviceIdType.MESH
            )

    for load in loads[1:6]:
        load.wait()
    wo_inverse = build_tables(wo_books, wo_tab)
    wo_scale[...] = wo_scale[...] * wo_inverse
    gate_inverse = build_tables(gate_books, gate_tab)
    gate_scale[...] = gate_scale_flat[...][None, :] * gate_inverse

    def unpack_wo(t):
        for u in range(Y):
            block = t * Y + u
            unpack_rows(wo_codes, wo_tab, wo_scale, w1, block, u * n_z + t)

    def unpack_gate(first, last):
        def step(t, carry):
            for u in range(2):
                block = t * 2 + u
                unpack_rows(gate_codes, gate_tab, gate_scale, w2, block, block)
            return carry

        lax.fori_loop(first // 2, last // 2, step, 0)

    unpack_wo(0)

    def relay_features(t, carry):
        tile = (z + offset(t, n_z)) % n_z
        remote(xt.at[y, z], xt.at[y, tile], a1s.at[0], a1r.at[tile], at_z(1)).wait_recv()
        for d in (1, 3, 2):
            a2(t, d).start()
        unpack_wo(t)
        return carry

    lax.fori_loop(1, n_z, relay_features, 0)
    loads[6].wait()
    loads[7].wait()
    loads[8].wait()
    residual = remote(res, res_in, rs, rr, {"inp": z, "out": inp * Y + y})

    @pl.when(jnp.logical_not(diagonal))
    def _():
        pl.semaphore_wait(ready, 1)
        residual.start()

    unpack_gate(0, early)

    def project(source, first):
        lhs = xt[source].reshape(n_z * 64, B)
        start = pl.multiple_of(source * (n_z * 64), n_z * 64)
        product = lax.dot_general(
            lhs, w1[pl.ds(start, n_z * 64), :], (((0,), (0,)), ((), ())), preferred_element_type=F32
        )
        if first:
            acc1[...] = product
        else:
            acc1[...] += product

    project(y, True)
    for d in (1, 3, 2):
        source = (y + d) % Y
        for t in range(n_z):
            remote(xt.at[y, t], xt.at[source, t], a2s.at[0, 0], a2r.at[source, t], at_y(d)).wait_recv()
        project(source, False)
    part1[...] = acc1[...].astype(BF16).reshape(part1.shape)

    def column(r):
        return {"inp": z, "out": r * Y + y}

    def b(t):
        r = (z + offset(t, n_z)) % n_z
        return remote(part1.at[r], in1.at[inp], bs.at[t], br.at[inp], column(r))

    for t in range(n_z - 1, 0, -1):
        b(t).start()

    @pl.when(diagonal)
    def _():
        in1[inp] = part1[z]

    @pl.when(jnp.logical_not(diagonal))
    def _():
        b(0).start()

    unpack_gate(early, early + middle)

    @pl.when(diagonal)
    def _():
        res_in[...] = res[...]

    @pl.when(jnp.logical_not(diagonal))
    def _():
        residual.wait_send()
        remote(res, res_in, rs, rr, column(inp)).wait_recv()

    for d in range(n_inp):
        source = (inp + d) % n_inp

        def wait_part():
            remote(part1.at[0], in1.at[source], bs.at[0], br.at[source], at_z(1)).wait_recv()

        if d == 0:
            pl.when(jnp.logical_not(diagonal))(wait_part)
        else:
            wait_part()
    total = in1[0].astype(F32)
    for d in range(1, n_inp):
        total = total + in1[d].astype(F32)
    hidden = res_in[...].astype(F32) + total
    gained = (hidden * gain[...]).astype(BF16)
    new = lax.broadcasted_iota(I32, (128, 128), 1)
    old = lax.broadcasted_iota(I32, (128, 128), 0)
    order = (old == 64 * (new // 64) + 8 * (new % 8) + (new % 64) // 8).astype(BF16)
    for n in range(gained.shape[1] // 128):
        x2[y, z, :, pl.ds(n * 128, 128)] = jnp.dot(
            gained[:, n * 128 : n * 128 + 128], order, preferred_element_type=F32
        ).astype(BF16)

    def c1(t):
        return remote(x2.at[y, z], x2.at[y, z], c1s.at[t], c1r.at[z], at_z(offset(t, n_z)))

    def c2(t, d):
        tile = (z + offset(t, n_z)) % n_z
        return remote(x2.at[y, tile], x2.at[y, tile], c2s.at[t, d], c2r.at[y, tile], at_y(d))

    for t in range(1, n_z):
        c1(t).start()
    for d in (1, 3, 2):
        c2(0, d).start()

    row = lax.broadcasted_iota(I32, (rows, 128), 0)
    lane = lax.broadcasted_iota(I32, (rows, 128), 1)
    squares = jnp.sum(hidden * hidden, axis=1, keepdims=True)
    squares_in[inp] = jnp.sum(jnp.where(row == lane, squares, 0.0), axis=0, keepdims=True)
    inp_sum = remote(squares_in.at[inp], squares_in.at[inp], qs, qr.at[inp], {"inp": z})
    pl.when(jnp.logical_not(diagonal))(inp_sum.start)
    stream_rows = in1.at[0]
    in1[0] = hidden.astype(BF16)

    def stream(d):
        target = {"inp": (inp + d) % n_inp, "out": inp * Y + y}
        return remote(stream_rows, stream_ref.at[row_slice(z)], sts.at[d], strr.at[z], target)

    @pl.when(diagonal)
    def _():
        stream_ref[row_slice(z), :] = hidden.astype(BF16)

    def y_sum(d):
        return remote(squares_y.at[y], squares_y.at[y], ys.at[d], yr.at[y], at_y(d))

    def z_sum(d):
        return remote(squares_all, squares_all, zs.at[d], zr, at_z(d))

    def relay_tiles(t, carry):
        tile = (z + offset(t, n_z)) % n_z
        remote(x2.at[y, z], x2.at[y, tile], c1s.at[0], c1r.at[tile], at_z(1)).wait_recv()
        for d in (1, 3, 2):
            c2(t, d).start()
        return carry

    lax.fori_loop(1, n_z, relay_tiles, 0)
    for d in range(1, n_inp):
        stream(d).start()
    pl.when(jnp.logical_not(diagonal))(stream(0).start)

    @pl.when(diagonal)
    def _():
        for d in range(1, n_inp):
            source = (inp + d) % n_inp
            remote(
                squares_in.at[inp], squares_in.at[source], qs, qr.at[source], at_inp(d)
            ).wait_recv()
        squares_y[y] = jnp.sum(squares_in[...], axis=0)
        for d in range(1, Y):
            y_sum(d).start()

    unpack_gate(early + middle, early + middle + late)

    depth = x2.shape[3]

    def gate_rows(source):
        return pl.ds(pl.multiple_of(source * depth, depth), depth)

    def arrived(d):
        source = (y + d) % Y
        if d:
            for t in range(n_z):
                remote(x2.at[y, t], x2.at[source, t], c2s.at[0, 0], c2r.at[source, t], at_y(d)).wait_recv()
        return source

    for d in (0, 1, 3):
        source = arrived(d)
        for start, width in blocks:
            columns = pl.ds(start, width)
            product = jnp.dot(
                x2[source].reshape(B, depth), w2[gate_rows(source), columns], preferred_element_type=F32
            ).reshape(n_x, 2, rows, width)
            if d:
                acc2[:, :, :, columns] += product
            else:
                acc2[:, :, :, columns] = product

    def d1(k):
        columns = pl.ds(*blocks[k])
        return remote(
            part2.at[:, :, columns], pair2.at[:, :, columns], d1s.at[k], d1r.at[k],
            {"inp": 2 * x + 1 - core},
        )

    def d2(k, d):
        columns = pl.ds(*blocks[k])
        return remote(
            send2.at[(x + d) % n_x, :, columns], in2.at[x, :, columns], d2s.at[k, d], d2r.at[k, x],
            {"inp": ((x + d) % n_x) * 2 + core},
        )

    source = arrived(2)
    for k, (start, width) in enumerate(blocks):
        columns = pl.ds(start, width)
        acc2[:, :, :, columns] += jnp.dot(
            x2[source].reshape(B, depth), w2[gate_rows(source), columns], preferred_element_type=F32
        ).reshape(n_x, 2, rows, width)
        part2[:, :, columns] = acc2[:, 1 - core, :, columns].astype(BF16)
        d1(k).start()
    for k, (start, width) in enumerate(blocks):
        columns = pl.ds(start, width)
        d1(k).wait_recv()
        both = acc2[:, core, :, columns] + pair2[:, :, columns].astype(F32)
        acc2[:, core, :, columns] = both
        send2[:, :, columns] = both.astype(BF16)
        for d in (2, 1, 3):
            d2(k, d).start()

    @pl.when(diagonal)
    def _():
        for d in range(1, Y):
            source = (y + d) % Y
            remote(squares_y.at[y], squares_y.at[source], ys.at[0], yr.at[source], at_y(d)).wait_recv()
        squares_all[...] = jnp.sum(squares_y[...], axis=0)
        for d in range(1, n_z):
            z_sum(d).start()

    for d in range(n_z):
        source = (z + d) % n_z

        def wait_stream():
            remote(
                stream_rows, stream_ref.at[row_slice(source)], sts.at[0], strr.at[source], at_z(1)
            ).wait_recv()

        if d == 0:
            pl.when(jnp.logical_not(diagonal))(wait_stream)
        else:
            wait_stream()

    @pl.when(jnp.logical_not(diagonal))
    def _():
        b(0).wait_send()
        stream(0).wait_send()
        inp_sum.wait_send()

    @pl.when(diagonal)
    def _():
        for d in range(1, Y):
            y_sum(d).wait_send()

    for d in range(1, n_inp):
        b(d).wait_send()
        stream(d).wait_send()

    def sent(t, carry):
        @pl.when(t > 0)
        def _():
            a1(t).wait_send()
            c1(t).wait_send()

        for d in (1, 3, 2):
            a2(t, d).wait_send()
            c2(t, d).wait_send()
        return carry

    lax.fori_loop(0, n_z, sent, 0)

    @pl.when(diagonal)
    def _():
        for d in range(1, n_z):
            z_sum(d).wait_send()

    @pl.when(jnp.logical_not(diagonal))
    def _():
        remote(squares_all, squares_all, zs.at[0], zr, at_z(1)).wait_recv()

    mean = squares_all[...] * (1.0 / (depth * Y * n_z))
    mean = jnp.sum(jnp.where(row == lane, mean, 0.0), axis=1, keepdims=True)
    factor = lax.rsqrt(mean + EPS)

    for k, (start, width) in enumerate(blocks):
        columns = pl.ds(start, width)
        total = acc2[x, core, :, columns]
        for d in (1, 3, 2):
            source = (x + d) % n_x
            remote(
                send2.at[x, :, columns], in2.at[source, :, columns], d2s.at[k, 0], d2r.at[k, source],
                {"inp": source * 2 + core},
            ).wait_recv()
            total = total + in2[source, :, columns].astype(F32)
        gate_ref[:, columns] = (total * factor).astype(BF16)
        d1(k).wait_send()
        for d in range(1, n_x):
            d2(k, d).wait_send()


def per_device(
    attention, residual, wo_codes, wo_books, wo_scale, norm_gain, gate_codes, gate_books, gate_scale
):
    n_inp, n_out = lax.axis_size("inp"), lax.axis_size("out")
    n_z, n_x = n_out // Y, n_inp // 2
    rows = B // n_inp
    width, gate_width = wo_codes.shape[2], gate_codes.shape[2]
    depth = wo_codes.shape[1] * GROUP
    blocks = ((0, 896), (896, 768))
    vmem = pl.BlockSpec(memory_space=pltpu.VMEM)
    hbm = pl.BlockSpec(memory_space=pltpu.HBM)
    dma = pltpu.SemaphoreType.DMA
    args = (
        attention.T, residual, wo_codes, jnp.swapaxes(wo_books, 1, 2), wo_scale[None, :],
        norm_gain.reshape(n_out, 1, width), gate_codes, jnp.swapaxes(gate_books, 1, 2), gate_scale,
    )
    held = [pltpu.VMEM(a.shape, a.dtype) for a in args]
    held[1] = pltpu.VMEM((rows, width), BF16)
    held[5] = pltpu.VMEM((1, width), F32)
    return pl.pallas_call(
        functools.partial(kernel, blocks=blocks, early=12, middle=16, late=4),
        out_shape=(
            jax.ShapeDtypeStruct((B, width), BF16),
            jax.ShapeDtypeStruct((rows, gate_width), BF16),
        ),
        in_specs=[hbm] * 9,
        out_specs=(vmem, vmem),
        scratch_shapes=[
            *held,
            pltpu.VMEM((1, gate_width), F32),
            pltpu.VMEM((2, 4, 2, 8, 128), I32),
            pltpu.VMEM((2, 4, 2, 8, 128), I32),
            pltpu.VMEM((Y, n_z, 64, B), BF16),
            pltpu.VMEM((depth, width), BF16),
            pltpu.VMEM((B, width), F32),
            pltpu.VMEM((n_inp, rows, width), BF16),
            pltpu.VMEM((n_inp, rows, width), BF16),
            pltpu.VMEM((Y, n_z, rows, width), BF16),
            pltpu.VMEM((depth, gate_width), BF16),
            pltpu.VMEM((n_x, 2, rows, gate_width), F32),
            pltpu.VMEM((n_x, rows, gate_width), BF16),
            pltpu.VMEM((n_x, rows, gate_width), BF16),
            pltpu.VMEM((n_x, rows, gate_width), BF16),
            pltpu.VMEM((n_x, rows, gate_width), BF16),
            pltpu.VMEM((n_inp, 1, 128), F32),
            pltpu.VMEM((Y, 1, 128), F32),
            pltpu.VMEM((1, 128), F32),
            pltpu.VMEM((rows, width), BF16),
            dma((9,)), pltpu.SemaphoreType.REGULAR,
            dma((n_z,)), dma((n_z,)),
            dma((n_z, Y)), dma((Y, n_z)),
            dma, dma,
            dma((n_z,)), dma((n_inp,)),
            dma((n_inp,)), dma((n_z,)),
            dma((n_z,)), dma((n_z,)),
            dma((n_z, Y)), dma((Y, n_z)),
            dma, dma((n_inp,)),
            dma((Y,)), dma((Y,)),
            dma((n_z,)), dma,
            dma((len(blocks),)), dma((len(blocks),)),
            dma((len(blocks), n_x)), dma((len(blocks), n_x)),
        ],
        compiler_params=pltpu.CompilerParams(
            collective_id=0, has_side_effects=True, vmem_limit_bytes=48 << 20
        ),
        name="step",
    )(*[pltpu.with_memory_space_constraint(a, pltpu.HBM) for a in args])


def solution(mesh):
    placed = (
        P(None, ("inp", "out")),
        P(None, "out"),
        P(None, "inp", "out"),
        P(),
        P("out"),
        P(),
        P(None, "inp", "out"),
        P(),
        P("out"),
    )
    return jax.shard_map(
        per_device,
        mesh=mesh,
        in_specs=placed,
        out_specs=(P(None, "out"), P("inp", "out")),
        check_vma=False,
    )
```

```python
import functools

import jax
import jax.numpy as jnp
from jax import lax
from jax.experimental import pallas as pl
from jax.experimental.pallas import tpu as pltpu
from jax.sharding import PartitionSpec as P

B = 128
BOOK = 256
GROUP = 8
Y = 4
EPS = 1e-05
F32 = jnp.float32
BF16 = jnp.bfloat16
I32 = jnp.int32


def remote(src, dst, send_sem, recv_sem, device):
    return pltpu.make_async_remote_copy(
        src_ref=src,
        dst_ref=dst,
        send_sem=send_sem,
        recv_sem=recv_sem,
        device_id=device,
        device_id_type=pl.DeviceIdType.MESH,
    )


def build_tables(books_ref, tab_ref):
    rows = [books_ref[b].astype(F32) for b in range(2)]
    top = jnp.maximum(jnp.abs(rows[0]), jnp.abs(rows[1]))
    top = jnp.max(jnp.max(top, axis=0, keepdims=True), axis=1, keepdims=True)
    scale = jnp.full((1, 1), 2.0**18, F32)
    inverse = jnp.full((1, 1), 2.0**-18, F32)
    for j in range(1, 33):
        fits = top <= 2.0 ** (-5 - j)
        scale = jnp.where(fits, 2.0 ** (18 + j), scale)
        inverse = jnp.where(fits, 2.0 ** (-18 - j), inverse)
    for b in range(2):
        whole = jnp.round(rows[b] * scale).astype(I32)
        for p in range(4):
            word = whole[2 * p : 2 * p + 1] * 65536 + whole[2 * p + 1 : 2 * p + 2]
            for h in range(2):
                tab_ref[b, p, h] = jnp.broadcast_to(word[:, 128 * h : 128 * h + 128], (8, 128))
    return inverse


def pick(table, index):
    return jnp.take_along_axis(table, index, axis=1, mode="promise_in_bounds")


def unpack_rows(codes_ref, tab_ref, scale_ref, weight_ref, block, place):
    tabs = [[[tab_ref[b, p, h] for h in range(2)] for p in range(4)] for b in range(2)]
    for n in range(codes_ref.shape[2] // 128):
        columns = pl.ds(n * 128, 128)
        scale = jnp.broadcast_to(scale_ref[:, columns], (16, 128))
        found = []
        for b in range(2):
            code = codes_ref[b, pl.ds(pl.multiple_of(block * 8, 8), 8), columns]
            low = code & 127
            first = code < 128
            found.append(
                [jnp.where(first, pick(tabs[b][p][0], low), pick(tabs[b][p][1], low)) for p in range(4)]
            )
        for p in range(4):
            word = found[0][p] + found[1][p]
            odd = (word << 16) >> 16
            even = (word - odd) >> 16
            pair = jnp.concatenate([even.astype(F32), odd.astype(F32)], axis=0) * scale
            start = pl.multiple_of(place * 64 + p * 16, 16)
            weight_ref[pl.ds(start, 16), columns] = pair.astype(BF16)


def rem(a, n):
    return a % n if isinstance(a, int) else lax.rem(a, n)


def div(a, n):
    return a // n if isinstance(a, int) else lax.div(a, n)


def offset(t, n):
    return rem(t, 2) * div(t + 1, 2) + (1 - rem(t, 2)) * rem(n - div(t, 2), n)


def kernel(
    att_hbm, res_hbm, wo_codes_hbm, wo_books_hbm, wo_scale_hbm, gain_hbm, gate_codes_hbm, gate_books_hbm,
    gate_scale_hbm,
    stream_ref, gate_ref,
    att, res, wo_codes, wo_books, wo_scale, gain, gate_codes, gate_books, gate_scale_flat,
    gate_scale, wo_tab, gate_tab, xt, w1, acc1, part1, in1, x2, w2, acc2, part2, pair2, send2, in2, squares_in, squares_y, squares_all, res_in,
    load_sem, ready, a1s, a1r, a2s, a2r, rs, rr, bs, br, sts, strr, c1s, c1r, c2s, c2r, qs, qr, ys, yr, zs, zr,
    d1s, d1r, d2s, d2r,
    *, blocks, early, middle, late,
):
    inp, out = lax.axis_index("inp"), lax.axis_index("out")
    n_inp, n_z = lax.axis_size("inp"), lax.axis_size("out") // Y
    n_x = n_inp // 2
    z, y, x, core = div(out, Y), rem(out, Y), div(inp, 2), rem(inp, 2)
    rows = B // n_inp
    diagonal = inp == z

    def row_slice(r):
        return pl.ds(pl.multiple_of(r * rows, rows), rows)

    def at_z(d):
        return {"out": (rem(z + d, n_z)) * Y + y}

    def at_y(d):
        return {"out": z * Y + rem(y + d, Y)}

    def at_inp(d):
        return {"inp": rem(inp + d, n_inp)}

    loads = [
        pltpu.make_async_copy(src, dst, load_sem.at[k])
        for k, (src, dst) in enumerate(
            (
                (att_hbm, att),
                (wo_books_hbm, wo_books),
                (wo_scale_hbm, wo_scale),
                (wo_codes_hbm, wo_codes),
                (gate_books_hbm, gate_books),
                (gate_scale_hbm, gate_scale_flat),
                (gate_codes_hbm, gate_codes),
                (res_hbm.at[row_slice(inp)], res),
                (gain_hbm.at[inp * Y + y], gain),
            )
        )
    ]
    loads[0].start()
    barrier = pltpu.get_barrier_semaphore()
    for at, n in ((at_z, n_z), (at_y, Y), (at_inp, n_inp)):
        for t in range(n - 1, 0, -1):
            pl.semaphore_signal(
                barrier, inc=1, device_id=at(offset(t, n)), device_id_type=pl.DeviceIdType.MESH
            )
    for load in loads[1:]:
        load.start()

    new = lax.broadcasted_iota(I32, (64, 64), 0)
    old = lax.broadcasted_iota(I32, (64, 64), 1)
    order = (old == 8 * (new % 8) + new // 8).astype(BF16)
    loads[0].wait()
    xt[y, z] = jnp.dot(order, att[...], preferred_element_type=F32).astype(BF16)
    pl.semaphore_wait(barrier, n_z + Y + n_inp - 3)

    def a1(t):
        d = offset(t, n_z)
        return remote(xt.at[y, z], xt.at[y, z], a1s, a1r.at[z], at_z(d))

    def a2(t, d):
        tile = rem(z + offset(t, n_z), n_z)
        return remote(xt.at[y, tile], xt.at[y, tile], a2s.at[d], a2r.at[y], at_y(d))

    for t in range(1, n_z):
        a1(t).start()
    for d in (1, 3, 2):
        a2(0, d).start()

    @pl.when(diagonal)
    def _():
        for d in range(1, n_inp):
            pl.semaphore_signal(
                ready, inc=1, device_id=at_inp(d), device_id_type=pl.DeviceIdType.MESH
            )

    for load in loads[1:4]:
        load.wait()
    wo_inverse = build_tables(wo_books, wo_tab)
    wo_scale[...] = wo_scale[...] * wo_inverse

    def unpack_wo(t):
        for u in range(Y):
            block = t * Y + u
            unpack_rows(wo_codes, wo_tab, wo_scale, w1, block, u * n_z + t)

    def unpack_gate(first, last):
        def step(t, carry):
            for u in range(2):
                block = t * 2 + u
                unpack_rows(gate_codes, gate_tab, gate_scale, w2, block, block)
            return carry

        lax.fori_loop(first // 2, last // 2, step, 0)

    unpack_wo(0)

    def relay_features(t, carry):
        tile = rem(z + offset(t, n_z), n_z)
        remote(xt.at[y, z], xt.at[y, tile], a1s, a1r.at[tile], at_z(1)).wait_recv()
        for d in (2, 1, 3):
            a2(t, d).start()
        unpack_wo(t)
        return carry

    lax.fori_loop(1, n_z, relay_features, 0)
    for load in loads[4:]:
        load.wait()
    gate_inverse = build_tables(gate_books, gate_tab)
    gate_scale[...] = gate_scale_flat[...][None, :] * gate_inverse
    residual = remote(res, res_in, rs, rr, {"inp": z, "out": inp * Y + y})

    @pl.when(jnp.logical_not(diagonal))
    def _():
        pl.semaphore_wait(ready, 1)
        residual.start()

    unpack_gate(0, early)

    def project(source, first):
        lhs = xt[source].reshape(n_z * 64, B)
        start = pl.multiple_of(source * (n_z * 64), n_z * 64)
        product = lax.dot_general(
            lhs, w1[pl.ds(start, n_z * 64), :], (((0,), (0,)), ((), ())), preferred_element_type=F32
        )
        if first:
            acc1[...] = product
        else:
            acc1[...] += product

    project(y, True)
    for d in (1, 3, 2):
        source = rem(y + d, Y)
        remote(xt.at[y], xt.at[source], a2s.at[0], a2r.at[source], at_y(d)).wait_recv()
        project(source, False)
    part1[...] = acc1[...].astype(BF16).reshape(part1.shape)

    def column(r):
        return {"inp": z, "out": r * Y + y}

    def b(t):
        r = rem(z + offset(t, n_z), n_z)
        return remote(part1.at[r], in1.at[inp], bs, br, column(r))

    for t in range(n_z - 1, 0, -1):
        b(t).start()

    @pl.when(diagonal)
    def _():
        in1[inp] = part1[z]

    @pl.when(jnp.logical_not(diagonal))
    def _():
        b(0).start()

    most = pl.ds(0, n_z - 1)
    remote(xt.at[y, most], xt.at[y, most], a1s, a1r.at[z], at_z(1)).wait_send()
    for d in range(1, Y):
        remote(xt.at[y], xt.at[y], a2s.at[d], a2r.at[y], at_y(d)).wait_send()
    unpack_gate(early, early + middle)

    @pl.when(diagonal)
    def _():
        res_in[...] = res[...]

    @pl.when(jnp.logical_not(diagonal))
    def _():
        residual.wait_send()
        remote(res, res_in, rs, rr, column(inp)).wait_recv()

    def parts(n):
        return remote(part1.at[pl.ds(0, n)], in1.at[pl.ds(0, n)], bs, br, at_z(1))

    @pl.when(diagonal)
    def _():
        parts(n_inp - 1).wait_recv()

    @pl.when(jnp.logical_not(diagonal))
    def _():
        parts(n_inp).wait_recv()

    total = in1[0].astype(F32)
    for d in range(1, n_inp):
        total = total + in1[d].astype(F32)
    hidden = res_in[...].astype(F32) + total
    gained = (hidden * gain[...]).astype(BF16)
    new = lax.broadcasted_iota(I32, (128, 128), 1)
    old = lax.broadcasted_iota(I32, (128, 128), 0)
    order = (old == 64 * (new // 64) + 8 * (new % 8) + (new % 64) // 8).astype(BF16)
    for n in range(gained.shape[1] // 128):
        x2[y, z, :, pl.ds(n * 128, 128)] = jnp.dot(
            gained[:, n * 128 : n * 128 + 128], order, preferred_element_type=F32
        ).astype(BF16)

    def c1(t):
        return remote(x2.at[y, z], x2.at[y, z], c1s, c1r.at[z], at_z(offset(t, n_z)))

    def c2(t, d):
        tile = rem(z + offset(t, n_z), n_z)
        return remote(x2.at[y, tile], x2.at[y, tile], c2s.at[d], c2r.at[y], at_y(d))

    for t in range(1, n_z):
        c1(t).start()
    for d in (1, 3, 2):
        c2(0, d).start()

    row = lax.broadcasted_iota(I32, (rows, 128), 0)
    lane = lax.broadcasted_iota(I32, (rows, 128), 1)
    squares = jnp.sum(hidden * hidden, axis=1, keepdims=True)
    squares_in[inp] = jnp.sum(jnp.where(row == lane, squares, 0.0), axis=0, keepdims=True)
    inp_sum = remote(squares_in.at[inp], squares_in.at[inp], qs, qr.at[inp], {"inp": z})
    pl.when(jnp.logical_not(diagonal))(inp_sum.start)
    stream_rows = in1.at[0]
    in1[0] = hidden.astype(BF16)

    def stream(d):
        target = {"inp": rem(inp + d, n_inp), "out": inp * Y + y}
        return remote(stream_rows, stream_ref.at[row_slice(z)], sts, strr, target)

    @pl.when(diagonal)
    def _():
        stream_ref[row_slice(z), :] = hidden.astype(BF16)

    def y_sum(d):
        return remote(squares_y.at[y], squares_y.at[y], ys.at[d], yr.at[y], at_y(d))

    def z_sum(d):
        return remote(squares_all, squares_all, zs.at[d], zr, at_z(d))

    for t in range(1, n_z):
        tile = rem(z + offset(t, n_z), n_z)
        remote(x2.at[y, z], x2.at[y, tile], c1s, c1r.at[tile], at_z(1)).wait_recv()
        for d in (2, 1, 3):
            c2(t, d).start()
    for d in range(1, n_inp):
        stream(d).start()
    pl.when(jnp.logical_not(diagonal))(stream(0).start)

    @pl.when(diagonal)
    def _():
        for d in range(1, n_inp):
            source = rem(inp + d, n_inp)
            remote(
                squares_in.at[inp], squares_in.at[source], qs, qr.at[source], at_inp(d)
            ).wait_recv()
        squares_y[y] = jnp.sum(squares_in[...], axis=0)
        for d in range(1, Y):
            y_sum(d).start()

    unpack_gate(early + middle, early + middle + late)

    depth = x2.shape[3]

    def gate_rows(source):
        return pl.ds(pl.multiple_of(source * depth, depth), depth)

    def arrived(d):
        source = rem(y + d, Y)
        if d:
            remote(x2.at[y], x2.at[source], c2s.at[0], c2r.at[source], at_y(d)).wait_recv()
        return source

    for d in (0, 1, 3):
        source = arrived(d)
        for start, width in blocks:
            columns = pl.ds(start, width)
            product = jnp.dot(
                x2[source].reshape(B, depth), w2[gate_rows(source), columns], preferred_element_type=F32
            ).reshape(n_x, 2, rows, width)
            if d:
                acc2[:, :, :, columns] += product
            else:
                acc2[:, :, :, columns] = product

    def d1(k):
        columns = pl.ds(*blocks[k])
        return remote(
            part2.at[:, :, columns], pair2.at[:, :, columns], d1s.at[k], d1r.at[k],
            {"inp": 2 * x + 1 - core},
        )

    def d2(k, d):
        columns = pl.ds(*blocks[k])
        return remote(
            send2.at[rem(x + d, n_x), :, columns], in2.at[x, :, columns], d2s.at[k, d], d2r.at[k, x],
            {"inp": (rem(x + d, n_x)) * 2 + core},
        )

    source = arrived(2)
    for k, (start, width) in enumerate(blocks):
        columns = pl.ds(start, width)
        acc2[:, :, :, columns] += jnp.dot(
            x2[source].reshape(B, depth), w2[gate_rows(source), columns], preferred_element_type=F32
        ).reshape(n_x, 2, rows, width)
        part2[:, :, columns] = acc2[:, 1 - core, :, columns].astype(BF16)
        d1(k).start()
    for k, (start, width) in enumerate(blocks):
        columns = pl.ds(start, width)
        d1(k).wait_recv()
        both = acc2[:, core, :, columns] + pair2[:, :, columns].astype(F32)
        send2[:, :, columns] = both.astype(BF16)
        for d in (2, 1, 3):
            d2(k, d).start()

    @pl.when(diagonal)
    def _():
        for d in range(1, Y):
            source = rem(y + d, Y)
            remote(squares_y.at[y], squares_y.at[source], ys.at[0], yr.at[source], at_y(d)).wait_recv()
        squares_all[...] = jnp.sum(squares_y[...], axis=0)
        for d in range(1, n_z):
            z_sum(d).start()

    def streams(n):
        there = stream_ref.at[pl.ds(0, n * rows)]
        return remote(there, there, sts, strr, at_z(1))

    @pl.when(jnp.logical_not(diagonal))
    def _():
        streams(n_inp).wait_recv()
        streams(n_inp).wait_send()
        parts(n_inp).wait_send()
        inp_sum.wait_send()

    @pl.when(diagonal)
    def _():
        streams(n_inp - 1).wait_recv()
        streams(n_inp - 1).wait_send()
        parts(n_inp - 1).wait_send()
        for d in range(1, Y):
            y_sum(d).wait_send()

    remote(x2.at[y, most], x2.at[y, most], c1s, c1r.at[z], at_z(1)).wait_send()
    for d in range(1, Y):
        remote(x2.at[y], x2.at[y], c2s.at[d], c2r.at[y], at_y(d)).wait_send()

    @pl.when(diagonal)
    def _():
        for d in range(1, n_z):
            z_sum(d).wait_send()

    @pl.when(jnp.logical_not(diagonal))
    def _():
        remote(squares_all, squares_all, zs.at[0], zr, at_z(1)).wait_recv()

    mean = squares_all[...] * (1.0 / (depth * Y * n_z))
    mean = jnp.sum(jnp.where(row == lane, mean, 0.0), axis=1, keepdims=True)
    factor = lax.rsqrt(mean + EPS)

    for k, (start, width) in enumerate(blocks):
        columns = pl.ds(start, width)
        total = acc2[x, core, :, columns] + pair2[x, :, columns].astype(F32)
        for d in (1, 3, 2):
            source = rem(x + d, n_x)
            remote(
                send2.at[x, :, columns], in2.at[source, :, columns], d2s.at[k, 0], d2r.at[k, source],
                {"inp": source * 2 + core},
            ).wait_recv()
            total = total + in2[source, :, columns].astype(F32)
        gate_ref[:, columns] = (total * factor).astype(BF16)
        d1(k).wait_send()
        for d in range(1, n_x):
            d2(k, d).wait_send()


def place(stream, gate, stream_out, gate_out, sem):
    copies = [
        pltpu.make_async_copy(stream, stream_out, sem.at[0]),
        pltpu.make_async_copy(gate, gate_out, sem.at[1]),
    ]
    for copy in copies:
        copy.start()
    for copy in copies:
        copy.wait()


def per_device(
    attention, residual, wo_codes, wo_books, wo_scale, norm_gain, gate_codes, gate_books, gate_scale
):
    n_inp, n_out = lax.axis_size("inp"), lax.axis_size("out")
    n_z, n_x = n_out // Y, n_inp // 2
    rows = B // n_inp
    width, gate_width = wo_codes.shape[2], gate_codes.shape[2]
    depth = wo_codes.shape[1] * GROUP
    blocks = ((0, 896), (896, 768))
    vmem = pl.BlockSpec(memory_space=pltpu.VMEM)
    hbm = pl.BlockSpec(memory_space=pltpu.HBM)
    dma = pltpu.SemaphoreType.DMA
    args = (
        attention.T, residual, wo_codes, jnp.swapaxes(wo_books, 1, 2), wo_scale[None, :],
        norm_gain.reshape(n_out, 1, width), gate_codes, jnp.swapaxes(gate_books, 1, 2), gate_scale,
    )
    held = [pltpu.VMEM(a.shape, a.dtype) for a in args]
    held[1] = pltpu.VMEM((rows, width), BF16)
    held[5] = pltpu.VMEM((1, width), F32)
    stream, gate = pl.pallas_call(
        functools.partial(kernel, blocks=blocks, early=8, middle=16, late=8),
        out_shape=(
            jax.ShapeDtypeStruct((B, width), BF16),
            jax.ShapeDtypeStruct((rows, gate_width), BF16),
        ),
        in_specs=[hbm] * 9,
        out_specs=(vmem, vmem),
        scratch_shapes=[
            *held,
            pltpu.VMEM((1, gate_width), F32),
            pltpu.VMEM((2, 4, 2, 8, 128), I32),
            pltpu.VMEM((2, 4, 2, 8, 128), I32),
            pltpu.VMEM((Y, n_z, 64, B), BF16),
            pltpu.VMEM((depth, width), BF16),
            pltpu.VMEM((B, width), F32),
            pltpu.VMEM((n_inp, rows, width), BF16),
            pltpu.VMEM((n_inp, rows, width), BF16),
            pltpu.VMEM((Y, n_z, rows, width), BF16),
            pltpu.VMEM((depth, gate_width), BF16),
            pltpu.VMEM((n_x, 2, rows, gate_width), F32),
            pltpu.VMEM((n_x, rows, gate_width), BF16),
            pltpu.VMEM((n_x, rows, gate_width), BF16),
            pltpu.VMEM((n_x, rows, gate_width), BF16),
            pltpu.VMEM((n_x, rows, gate_width), BF16),
            pltpu.VMEM((n_inp, 1, 128), F32),
            pltpu.VMEM((Y, 1, 128), F32),
            pltpu.VMEM((1, 128), F32),
            pltpu.VMEM((rows, width), BF16),
            dma((9,)), pltpu.SemaphoreType.REGULAR,
            dma, dma((n_z,)),
            dma((Y,)), dma((Y,)),
            dma, dma,
            dma, dma,
            dma, dma,
            dma, dma((n_z,)),
            dma((Y,)), dma((Y,)),
            dma, dma((n_inp,)),
            dma((Y,)), dma((Y,)),
            dma((n_z,)), dma,
            dma((len(blocks),)), dma((len(blocks),)),
            dma((len(blocks), n_x)), dma((len(blocks), n_x)),
        ],
        compiler_params=pltpu.CompilerParams(
            collective_id=0, has_side_effects=True, vmem_limit_bytes=48 << 20
        ),
        name="step",
    )(*[pltpu.with_memory_space_constraint(a, pltpu.HBM) for a in args])
    return pl.pallas_call(
        place,
        out_shape=(
            jax.ShapeDtypeStruct(stream.shape, BF16),
            jax.ShapeDtypeStruct(gate.shape, BF16),
        ),
        in_specs=[vmem, vmem],
        out_specs=(hbm, hbm),
        scratch_shapes=[dma((2,))],
        compiler_params=pltpu.CompilerParams(vmem_limit_bytes=4 << 20),
        name="place",
    )(stream, gate)


def solution(mesh):
    placed = (
        P(None, ("inp", "out")),
        P(None, "out"),
        P(None, "inp", "out"),
        P(),
        P("out"),
        P(),
        P(None, "inp", "out"),
        P(),
        P("out"),
    )
    return jax.shard_map(
        per_device,
        mesh=mesh,
        in_specs=placed,
        out_specs=(P(None, "out"), P("inp", "out")),
        check_vma=False,
    )
```

```python
import functools

import jax
import jax.numpy as jnp
from jax import lax
from jax.experimental import pallas as pl
from jax.experimental.pallas import tpu as pltpu
from jax.sharding import PartitionSpec as P

B = 128
BOOK = 256
GROUP = 8
Y = 4
EPS = 1e-05
F32 = jnp.float32
BF16 = jnp.bfloat16
I32 = jnp.int32


def remote(src, dst, send_sem, recv_sem, device):
    return pltpu.make_async_remote_copy(
        src_ref=src,
        dst_ref=dst,
        send_sem=send_sem,
        recv_sem=recv_sem,
        device_id=device,
        device_id_type=pl.DeviceIdType.MESH,
    )


def build_tables(books_ref, tab_ref):
    rows = [books_ref[b].astype(F32) for b in range(2)]
    top = jnp.maximum(jnp.abs(rows[0]), jnp.abs(rows[1]))
    top = jnp.max(jnp.max(top, axis=0, keepdims=True), axis=1, keepdims=True)
    scale = jnp.full((1, 1), 2.0**18, F32)
    inverse = jnp.full((1, 1), 2.0**-18, F32)
    for j in range(1, 33):
        fits = top <= 2.0 ** (-5 - j)
        scale = jnp.where(fits, 2.0 ** (18 + j), scale)
        inverse = jnp.where(fits, 2.0 ** (-18 - j), inverse)
    for b in range(2):
        whole = jnp.round(rows[b] * scale).astype(I32)
        for p in range(4):
            word = whole[2 * p : 2 * p + 1] * 65536 + whole[2 * p + 1 : 2 * p + 2]
            for h in range(2):
                tab_ref[b, p, h] = jnp.broadcast_to(word[:, 128 * h : 128 * h + 128], (8, 128))
    return inverse


def pick(table, index):
    return jnp.take_along_axis(table, index, axis=1, mode="promise_in_bounds")


def unpack_rows(codes_ref, tab_ref, scale_ref, weight_ref, block, place):
    tabs = [[[tab_ref[b, p, h] for h in range(2)] for p in range(4)] for b in range(2)]
    for n in range(codes_ref.shape[2] // 128):
        columns = pl.ds(n * 128, 128)
        scale = jnp.broadcast_to(scale_ref[:, columns], (16, 128))
        found = []
        for b in range(2):
            code = codes_ref[b, pl.ds(pl.multiple_of(block * 8, 8), 8), columns]
            low = code & 127
            first = code < 128
            found.append(
                [jnp.where(first, pick(tabs[b][p][0], low), pick(tabs[b][p][1], low)) for p in range(4)]
            )
        for p in range(4):
            word = found[0][p] + found[1][p]
            odd = (word << 16) >> 16
            even = (word - odd) >> 16
            pair = jnp.concatenate([even.astype(F32), odd.astype(F32)], axis=0) * scale
            start = pl.multiple_of(place * 64 + p * 16, 16)
            weight_ref[pl.ds(start, 16), columns] = pair.astype(BF16)


def rem(a, n):
    return a % n if isinstance(a, int) else lax.rem(a, n)


def div(a, n):
    return a // n if isinstance(a, int) else lax.div(a, n)


def offset(t, n):
    return rem(t, 2) * div(t + 1, 2) + (1 - rem(t, 2)) * rem(n - div(t, 2), n)


def kernel(
    att_hbm, res_hbm, wo_codes_hbm, wo_books_hbm, wo_scale_hbm, gain_hbm, gate_codes_hbm, gate_books_hbm,
    gate_scale_hbm,
    stream_ref, gate_ref,
    att, res, wo_codes, wo_books, wo_scale, gain, gate_codes, gate_books, gate_scale_flat,
    gate_scale, wo_tab, gate_tab, xt, w1, acc1, part1, in1, x2, w2, acc2, part2, pair2, send2, in2, squares_in, squares_y, squares_all, res_in,
    load_sem, ready, a1s, a1r, a2s, a2r, rs, rr, bs, br, sts, strr, c1s, c1r, c2s, c2r, qs, qr, ys, yr, zs, zr,
    d1s, d1r, d2s, d2r,
    *, blocks, early, middle, late,
):
    inp, out = lax.axis_index("inp"), lax.axis_index("out")
    n_inp, n_z = lax.axis_size("inp"), lax.axis_size("out") // Y
    n_x = n_inp // 2
    z, y, x, core = div(out, Y), rem(out, Y), div(inp, 2), rem(inp, 2)
    rows = B // n_inp
    diagonal = inp == z

    def row_slice(r):
        return pl.ds(pl.multiple_of(r * rows, rows), rows)

    def at_z(d):
        return {"out": (rem(z + d, n_z)) * Y + y}

    def at_y(d):
        return {"out": z * Y + rem(y + d, Y)}

    def at_inp(d):
        return {"inp": rem(inp + d, n_inp)}

    loads = [
        pltpu.make_async_copy(src, dst, load_sem.at[k])
        for k, (src, dst) in enumerate(
            (
                (att_hbm, att),
                (wo_books_hbm, wo_books),
                (wo_scale_hbm, wo_scale),
                (wo_codes_hbm, wo_codes),
                (gate_books_hbm, gate_books),
                (gate_scale_hbm, gate_scale_flat),
                (gate_codes_hbm, gate_codes),
                (res_hbm.at[row_slice(inp)], res),
                (gain_hbm.at[inp * Y + y], gain),
            )
        )
    ]
    loads[0].start()
    barrier = pltpu.get_barrier_semaphore()
    for at, n in ((at_z, n_z), (at_y, Y), (at_inp, n_inp)):
        for t in range(n - 1, 0, -1):
            pl.semaphore_signal(
                barrier, inc=1, device_id=at(offset(t, n)), device_id_type=pl.DeviceIdType.MESH
            )
    for load in loads[1:]:
        load.start()

    new = lax.broadcasted_iota(I32, (64, 64), 0)
    old = lax.broadcasted_iota(I32, (64, 64), 1)
    order = (old == 8 * (new % 8) + new // 8).astype(BF16)
    loads[0].wait()
    xt[y, z] = jnp.dot(order, att[...], preferred_element_type=F32).astype(BF16)
    pl.semaphore_wait(barrier, n_z + Y + n_inp - 3)

    def a1(t):
        d = offset(t, n_z)
        return remote(xt.at[y, z], xt.at[y, z], a1s, a1r.at[z], at_z(d))

    def a2(t, d):
        tile = rem(z + offset(t, n_z), n_z)
        return remote(xt.at[y, tile], xt.at[y, tile], a2s.at[d], a2r.at[y], at_y(d))

    for t in range(1, n_z):
        a1(t).start()
    for d in (1, 3, 2):
        a2(0, d).start()

    @pl.when(diagonal)
    def _():
        for d in range(1, n_inp):
            pl.semaphore_signal(
                ready, inc=1, device_id=at_inp(d), device_id_type=pl.DeviceIdType.MESH
            )

    for load in loads[1:4]:
        load.wait()
    wo_inverse = build_tables(wo_books, wo_tab)
    wo_scale[...] = wo_scale[...] * wo_inverse

    def unpack_wo(t):
        for u in range(Y):
            block = t * Y + u
            unpack_rows(wo_codes, wo_tab, wo_scale, w1, block, u * n_z + t)

    def unpack_gate(first, last):
        def step(t, carry):
            for u in range(4):
                block = t * 4 + u
                unpack_rows(gate_codes, gate_tab, gate_scale, w2, block, block)
            return carry

        lax.fori_loop(first // 4, last // 4, step, 0)

    unpack_wo(0)

    def relay_features(t, carry):
        tile = rem(z + offset(t, n_z), n_z)
        remote(xt.at[y, z], xt.at[y, tile], a1s, a1r.at[tile], at_z(1)).wait_recv()
        for d in (2, 1, 3):
            a2(t, d).start()
        unpack_wo(t)
        return carry

    lax.fori_loop(1, n_z, relay_features, 0)
    for load in loads[4:]:
        load.wait()
    gate_inverse = build_tables(gate_books, gate_tab)
    gate_scale[...] = gate_scale_flat[...][None, :] * gate_inverse
    residual = remote(res, res_in, rs, rr, {"inp": z, "out": inp * Y + y})

    @pl.when(jnp.logical_not(diagonal))
    def _():
        pl.semaphore_wait(ready, 1)
        residual.start()

    unpack_gate(0, early)

    def project(source):
        lhs = xt[source].reshape(n_z * 64, B)
        start = pl.multiple_of(source * (n_z * 64), n_z * 64)
        return lax.dot_general(
            lhs, w1[pl.ds(start, n_z * 64), :], (((0,), (0,)), ((), ())), preferred_element_type=F32
        )

    acc1[...] = project(y)
    for d in (1, 3, 2):
        source = rem(y + d, Y)
        remote(xt.at[y], xt.at[source], a2s.at[0], a2r.at[source], at_y(d)).wait_recv()
        if d == 2:
            part1[...] = (acc1[...] + project(source)).astype(BF16).reshape(part1.shape)
        else:
            acc1[...] += project(source)

    def column(r):
        return {"inp": z, "out": r * Y + y}

    def b(t):
        r = rem(z + offset(t, n_z), n_z)
        return remote(part1.at[r], in1.at[inp], bs, br, column(r))

    for t in range(n_z - 1, 0, -1):
        b(t).start()

    @pl.when(diagonal)
    def _():
        in1[inp] = part1[z]

    @pl.when(jnp.logical_not(diagonal))
    def _():
        b(0).start()

    most = pl.ds(0, n_z - 1)
    remote(xt.at[y, most], xt.at[y, most], a1s, a1r.at[z], at_z(1)).wait_send()
    for d in range(1, Y):
        remote(xt.at[y], xt.at[y], a2s.at[d], a2r.at[y], at_y(d)).wait_send()
    unpack_gate(early, early + middle)

    @pl.when(diagonal)
    def _():
        res_in[...] = res[...]

    @pl.when(jnp.logical_not(diagonal))
    def _():
        residual.wait_send()
        remote(res, res_in, rs, rr, column(inp)).wait_recv()

    def parts(n):
        return remote(part1.at[pl.ds(0, n)], in1.at[pl.ds(0, n)], bs, br, at_z(1))

    @pl.when(diagonal)
    def _():
        parts(n_inp - 1).wait_recv()

    @pl.when(jnp.logical_not(diagonal))
    def _():
        parts(n_inp).wait_recv()

    total = in1[0].astype(F32)
    for d in range(1, n_inp):
        total = total + in1[d].astype(F32)
    hidden = res_in[...].astype(F32) + total
    gained = hidden * gain[...]
    new = lax.broadcasted_iota(I32, (8, 128), 1)
    order = 64 * (new // 64) + 8 * (new % 8) + (new % 64) // 8
    for n in range(gained.shape[1] // 128):
        columns = slice(n * 128, n * 128 + 128)
        moved = [pick(gained[8 * h : 8 * h + 8, columns], order) for h in range(rows // 8)]
        x2[y, z, :, columns] = jnp.concatenate(moved, axis=0).astype(BF16)

    def c1(t):
        return remote(x2.at[y, z], x2.at[y, z], c1s, c1r.at[z], at_z(offset(t, n_z)))

    def c2(t, d):
        tile = rem(z + offset(t, n_z), n_z)
        return remote(x2.at[y, tile], x2.at[y, tile], c2s.at[d], c2r.at[y], at_y(d))

    for t in range(1, n_z):
        c1(t).start()
    for d in (1, 3, 2):
        c2(0, d).start()

    row = lax.broadcasted_iota(I32, (rows, 128), 0)
    lane = lax.broadcasted_iota(I32, (rows, 128), 1)
    squares = jnp.sum(hidden * hidden, axis=1, keepdims=True)
    squares_in[inp] = jnp.sum(jnp.where(row == lane, squares, 0.0), axis=0, keepdims=True)
    inp_sum = remote(squares_in.at[inp], squares_in.at[inp], qs, qr.at[inp], {"inp": z})
    pl.when(jnp.logical_not(diagonal))(inp_sum.start)
    stream_rows = in1.at[0]
    in1[0] = hidden.astype(BF16)

    def stream(d):
        target = {"inp": rem(inp + d, n_inp), "out": inp * Y + y}
        return remote(stream_rows, stream_ref.at[row_slice(z)], sts, strr, target)

    @pl.when(diagonal)
    def _():
        stream_ref[row_slice(z), :] = hidden.astype(BF16)

    def y_sum(d):
        return remote(squares_y.at[y], squares_y.at[y], ys.at[d], yr.at[y], at_y(d))

    def z_sum(d):
        return remote(squares_all, squares_all, zs.at[d], zr, at_z(d))

    for t in range(1, n_z):
        tile = rem(z + offset(t, n_z), n_z)
        remote(x2.at[y, z], x2.at[y, tile], c1s, c1r.at[tile], at_z(1)).wait_recv()
        for d in (2, 1, 3):
            c2(t, d).start()
    for d in range(1, n_inp):
        stream(d).start()
    pl.when(jnp.logical_not(diagonal))(stream(0).start)

    @pl.when(diagonal)
    def _():
        for d in range(1, n_inp):
            source = rem(inp + d, n_inp)
            remote(
                squares_in.at[inp], squares_in.at[source], qs, qr.at[source], at_inp(d)
            ).wait_recv()
        squares_y[y] = jnp.sum(squares_in[...], axis=0)
        for d in range(1, Y):
            y_sum(d).start()

    unpack_gate(early + middle, early + middle + late)

    depth = x2.shape[3]

    def gate_rows(source):
        return pl.ds(pl.multiple_of(source * depth, depth), depth)

    def arrived(d):
        source = rem(y + d, Y)
        if d:
            remote(x2.at[y], x2.at[source], c2s.at[0], c2r.at[source], at_y(d)).wait_recv()
        return source

    for d in (0, 1, 3):
        source = arrived(d)
        for start, width in blocks:
            columns = pl.ds(start, width)
            product = jnp.dot(
                x2[source].reshape(B, depth), w2[gate_rows(source), columns], preferred_element_type=F32
            ).reshape(n_x, 2, rows, width)
            if d:
                acc2[:, :, :, columns] += product
            else:
                acc2[:, :, :, columns] = product

    def d1(k):
        columns = pl.ds(*blocks[k])
        return remote(
            part2.at[:, :, columns], pair2.at[:, :, columns], d1s.at[k], d1r.at[k],
            {"inp": 2 * x + 1 - core},
        )

    def d2(k, d):
        columns = pl.ds(*blocks[k])
        return remote(
            send2.at[rem(x + d, n_x), :, columns], in2.at[x, :, columns], d2s.at[k, d], d2r.at[k, x],
            {"inp": (rem(x + d, n_x)) * 2 + core},
        )

    source = arrived(2)
    for k, (start, width) in enumerate(blocks):
        columns = pl.ds(start, width)
        acc2[:, :, :, columns] += jnp.dot(
            x2[source].reshape(B, depth), w2[gate_rows(source), columns], preferred_element_type=F32
        ).reshape(n_x, 2, rows, width)
        part2[:, :, columns] = acc2[:, 1 - core, :, columns].astype(BF16)
        d1(k).start()
    for k, (start, width) in enumerate(blocks):
        columns = pl.ds(start, width)
        d1(k).wait_recv()
        both = acc2[:, core, :, columns] + pair2[:, :, columns].astype(F32)
        send2[:, :, columns] = both.astype(BF16)
        for d in (2, 1, 3):
            d2(k, d).start()

    @pl.when(diagonal)
    def _():
        for d in range(1, Y):
            source = rem(y + d, Y)
            remote(squares_y.at[y], squares_y.at[source], ys.at[0], yr.at[source], at_y(d)).wait_recv()
        squares_all[...] = jnp.sum(squares_y[...], axis=0)
        for d in range(1, n_z):
            z_sum(d).start()

    def streams(n):
        there = stream_ref.at[pl.ds(0, n * rows)]
        return remote(there, there, sts, strr, at_z(1))

    @pl.when(jnp.logical_not(diagonal))
    def _():
        streams(n_inp).wait_recv()
        streams(n_inp).wait_send()
        parts(n_inp).wait_send()
        inp_sum.wait_send()

    @pl.when(diagonal)
    def _():
        streams(n_inp - 1).wait_recv()
        streams(n_inp - 1).wait_send()
        parts(n_inp - 1).wait_send()
        for d in range(1, Y):
            y_sum(d).wait_send()

    remote(x2.at[y, most], x2.at[y, most], c1s, c1r.at[z], at_z(1)).wait_send()
    for d in range(1, Y):
        remote(x2.at[y], x2.at[y], c2s.at[d], c2r.at[y], at_y(d)).wait_send()

    @pl.when(diagonal)
    def _():
        for d in range(1, n_z):
            z_sum(d).wait_send()

    @pl.when(jnp.logical_not(diagonal))
    def _():
        remote(squares_all, squares_all, zs.at[0], zr, at_z(1)).wait_recv()

    mean = squares_all[...] * (1.0 / (depth * Y * n_z))
    mean = jnp.sum(jnp.where(row == lane, mean, 0.0), axis=1, keepdims=True)
    factor = lax.rsqrt(mean + EPS)

    for k, (start, width) in enumerate(blocks):
        columns = pl.ds(start, width)
        total = acc2[x, core, :, columns] + pair2[x, :, columns].astype(F32)
        for d in (1, 3, 2):
            source = rem(x + d, n_x)
            remote(
                send2.at[x, :, columns], in2.at[source, :, columns], d2s.at[k, 0], d2r.at[k, source],
                {"inp": source * 2 + core},
            ).wait_recv()
            total = total + in2[source, :, columns].astype(F32)
        gate_ref[:, columns] = (total * factor).astype(BF16)
        d1(k).wait_send()
        for d in range(1, n_x):
            d2(k, d).wait_send()


def place(stream, gate, stream_out, gate_out, sem):
    copies = [
        pltpu.make_async_copy(stream, stream_out, sem.at[0]),
        pltpu.make_async_copy(gate, gate_out, sem.at[1]),
    ]
    for copy in copies:
        copy.start()
    for copy in copies:
        copy.wait()


def per_device(
    attention, residual, wo_codes, wo_books, wo_scale, norm_gain, gate_codes, gate_books, gate_scale
):
    n_inp, n_out = lax.axis_size("inp"), lax.axis_size("out")
    n_z, n_x = n_out // Y, n_inp // 2
    rows = B // n_inp
    width, gate_width = wo_codes.shape[2], gate_codes.shape[2]
    depth = wo_codes.shape[1] * GROUP
    blocks = ((0, 896), (896, 768))
    vmem = pl.BlockSpec(memory_space=pltpu.VMEM)
    hbm = pl.BlockSpec(memory_space=pltpu.HBM)
    dma = pltpu.SemaphoreType.DMA
    args = (
        attention.T, residual, wo_codes, jnp.swapaxes(wo_books, 1, 2), wo_scale[None, :],
        norm_gain.reshape(n_out, 1, width), gate_codes, jnp.swapaxes(gate_books, 1, 2), gate_scale,
    )
    held = [pltpu.VMEM(a.shape, a.dtype) for a in args]
    held[1] = pltpu.VMEM((rows, width), BF16)
    held[5] = pltpu.VMEM((1, width), F32)
    stream, gate = pl.pallas_call(
        functools.partial(kernel, blocks=blocks, early=8, middle=16, late=8),
        out_shape=(
            jax.ShapeDtypeStruct((B, width), BF16),
            jax.ShapeDtypeStruct((rows, gate_width), BF16),
        ),
        in_specs=[hbm] * 9,
        out_specs=(vmem, vmem),
        scratch_shapes=[
            *held,
            pltpu.VMEM((1, gate_width), F32),
            pltpu.VMEM((2, 4, 2, 8, 128), I32),
            pltpu.VMEM((2, 4, 2, 8, 128), I32),
            pltpu.VMEM((Y, n_z, 64, B), BF16),
            pltpu.VMEM((depth, width), BF16),
            pltpu.VMEM((B, width), F32),
            pltpu.VMEM((n_inp, rows, width), BF16),
            pltpu.VMEM((n_inp, rows, width), BF16),
            pltpu.VMEM((Y, n_z, rows, width), BF16),
            pltpu.VMEM((depth, gate_width), BF16),
            pltpu.VMEM((n_x, 2, rows, gate_width), F32),
            pltpu.VMEM((n_x, rows, gate_width), BF16),
            pltpu.VMEM((n_x, rows, gate_width), BF16),
            pltpu.VMEM((n_x, rows, gate_width), BF16),
            pltpu.VMEM((n_x, rows, gate_width), BF16),
            pltpu.VMEM((n_inp, 1, 128), F32),
            pltpu.VMEM((Y, 1, 128), F32),
            pltpu.VMEM((1, 128), F32),
            pltpu.VMEM((rows, width), BF16),
            dma((9,)), pltpu.SemaphoreType.REGULAR,
            dma, dma((n_z,)),
            dma((Y,)), dma((Y,)),
            dma, dma,
            dma, dma,
            dma, dma,
            dma, dma((n_z,)),
            dma((Y,)), dma((Y,)),
            dma, dma((n_inp,)),
            dma((Y,)), dma((Y,)),
            dma((n_z,)), dma,
            dma((len(blocks),)), dma((len(blocks),)),
            dma((len(blocks), n_x)), dma((len(blocks), n_x)),
        ],
        compiler_params=pltpu.CompilerParams(
            collective_id=0, has_side_effects=True, vmem_limit_bytes=48 << 20
        ),
        name="step",
    )(*[pltpu.with_memory_space_constraint(a, pltpu.HBM) for a in args])
    return pl.pallas_call(
        place,
        out_shape=(
            jax.ShapeDtypeStruct(stream.shape, BF16),
            jax.ShapeDtypeStruct(gate.shape, BF16),
        ),
        in_specs=[vmem, vmem],
        out_specs=(hbm, hbm),
        scratch_shapes=[dma((2,))],
        compiler_params=pltpu.CompilerParams(vmem_limit_bytes=4 << 20),
        name="place",
    )(stream, gate)


def solution(mesh):
    placed = (
        P(None, ("inp", "out")),
        P(None, "out"),
        P(None, "inp", "out"),
        P(),
        P("out"),
        P(),
        P(None, "inp", "out"),
        P(),
        P("out"),
    )
    return jax.shard_map(
        per_device,
        mesh=mesh,
        in_specs=placed,
        out_specs=(P(None, "out"), P("inp", "out")),
        check_vma=False,
    )
```

```python
import functools

import jax
import jax.numpy as jnp
from jax import lax
from jax.experimental import pallas as pl
from jax.experimental.pallas import tpu as pltpu
from jax.sharding import PartitionSpec as P

B = 128
BOOK = 256
GROUP = 8
Y = 4
EPS = 1e-05
F32 = jnp.float32
BF16 = jnp.bfloat16
I32 = jnp.int32


def remote(src, dst, send_sem, recv_sem, device):
    return pltpu.make_async_remote_copy(
        src_ref=src,
        dst_ref=dst,
        send_sem=send_sem,
        recv_sem=recv_sem,
        device_id=device,
        device_id_type=pl.DeviceIdType.MESH,
    )


def build_tables(books_ref, tab_ref):
    rows = [books_ref[b].astype(F32) for b in range(2)]
    top = jnp.maximum(jnp.abs(rows[0]), jnp.abs(rows[1]))
    top = jnp.max(jnp.max(top, axis=0, keepdims=True), axis=1, keepdims=True)
    scale = jnp.full((1, 1), 2.0**18, F32)
    inverse = jnp.full((1, 1), 2.0**-18, F32)
    for j in range(1, 33):
        fits = top <= 2.0 ** (-5 - j)
        scale = jnp.where(fits, 2.0 ** (18 + j), scale)
        inverse = jnp.where(fits, 2.0 ** (-18 - j), inverse)
    for b in range(2):
        whole = jnp.round(rows[b] * scale).astype(I32)
        for p in range(4):
            word = whole[2 * p : 2 * p + 1] * 65536 + whole[2 * p + 1 : 2 * p + 2]
            for h in range(2):
                tab_ref[b, p, h] = jnp.broadcast_to(word[:, 128 * h : 128 * h + 128], (8, 128))
    return inverse


def pick(table, index):
    return jnp.take_along_axis(table, index, axis=1, mode="promise_in_bounds")


def unpack_rows(codes_ref, tab_ref, scale_ref, weight_ref, block, place):
    tabs = [[[tab_ref[b, p, h] for h in range(2)] for p in range(4)] for b in range(2)]
    for n in range(codes_ref.shape[2] // 128):
        columns = pl.ds(n * 128, 128)
        scale = jnp.broadcast_to(scale_ref[:, columns], (16, 128))
        found = []
        for b in range(2):
            code = codes_ref[b, pl.ds(pl.multiple_of(block * 8, 8), 8), columns]
            low = code & 127
            first = code < 128
            found.append(
                [jnp.where(first, pick(tabs[b][p][0], low), pick(tabs[b][p][1], low)) for p in range(4)]
            )
        for p in range(4):
            word = found[0][p] + found[1][p]
            odd = (word << 16) >> 16
            even = (word - odd) >> 16
            pair = jnp.concatenate([even.astype(F32), odd.astype(F32)], axis=0) * scale
            start = pl.multiple_of(place * 64 + p * 16, 16)
            weight_ref[pl.ds(start, 16), columns] = pair.astype(BF16)


def rem(a, n):
    return a % n if isinstance(a, int) else lax.rem(a, n)


def div(a, n):
    return a // n if isinstance(a, int) else lax.div(a, n)


def offset(t, n):
    return rem(t, 2) * div(t + 1, 2) + (1 - rem(t, 2)) * rem(n - div(t, 2), n)


def kernel(
    att_hbm, res_hbm, wo_codes_hbm, wo_books_hbm, wo_scale_hbm, gain_hbm, gate_codes_hbm, gate_books_hbm,
    gate_scale_hbm,
    stream_ref, gate_ref,
    att, res, wo_codes, wo_books, wo_scale, gain, gate_codes, gate_books, gate_scale_flat,
    gate_scale, wo_tab, gate_tab, xt, w1, acc1, part1, in1, x2, w2, acc2, part2, pair2, send2, in2, squares_in, squares_y, squares_all, res_in,
    load_sem, ready, a1s, a1r, a2s, a2r, rs, rr, bs, br, sts, strr, c1s, c1r, c2s, c2r, qs, qr, ys, yr, zs, zr,
    d1s, d1r, d2s, d2r,
    *, blocks, early, middle, late,
):
    inp, out = lax.axis_index("inp"), lax.axis_index("out")
    n_inp, n_z = lax.axis_size("inp"), lax.axis_size("out") // Y
    n_x = n_inp // 2
    z, y, x, core = div(out, Y), rem(out, Y), div(inp, 2), rem(inp, 2)
    rows = B // n_inp
    diagonal = inp == z

    def row_slice(r):
        return pl.ds(pl.multiple_of(r * rows, rows), rows)

    def at_z(d):
        return {"out": (rem(z + d, n_z)) * Y + y}

    def at_y(d):
        return {"out": z * Y + rem(y + d, Y)}

    def at_inp(d):
        return {"inp": rem(inp + d, n_inp)}

    loads = [
        pltpu.make_async_copy(src, dst, load_sem.at[k])
        for k, (src, dst) in enumerate(
            (
                (att_hbm, att),
                (wo_books_hbm, wo_books),
                (wo_scale_hbm, wo_scale),
                (wo_codes_hbm, wo_codes),
                (gate_books_hbm, gate_books),
                (gate_scale_hbm, gate_scale_flat),
                (gate_codes_hbm, gate_codes),
                (res_hbm.at[row_slice(inp)], res),
                (gain_hbm.at[inp * Y + y], gain),
            )
        )
    ]
    loads[0].start()
    barrier = pltpu.get_barrier_semaphore()
    for at, n in ((at_z, n_z), (at_y, Y), (at_inp, n_inp)):
        for t in range(n - 1, 0, -1):
            pl.semaphore_signal(
                barrier, inc=1, device_id=at(offset(t, n)), device_id_type=pl.DeviceIdType.MESH
            )
    for load in loads[1:]:
        load.start()

    new = lax.broadcasted_iota(I32, (64, 64), 0)
    old = lax.broadcasted_iota(I32, (64, 64), 1)
    order = (old == 8 * (new % 8) + new // 8).astype(BF16)
    loads[0].wait()
    xt[y, z] = jnp.dot(order, att[...], preferred_element_type=F32).astype(BF16)
    pl.semaphore_wait(barrier, n_z + Y + n_inp - 3)

    def a1(t):
        d = offset(t, n_z)
        return remote(xt.at[y, z], xt.at[y, z], a1s, a1r.at[z], at_z(d))

    def a2(t, d):
        tile = rem(z + offset(t, n_z), n_z)
        return remote(xt.at[y, tile], xt.at[y, tile], a2s.at[d], a2r.at[y], at_y(d))

    for t in range(1, n_z):
        a1(t).start()
    for d in (1, 3, 2):
        a2(0, d).start()

    @pl.when(diagonal)
    def _():
        for d in range(1, n_inp):
            pl.semaphore_signal(
                ready, inc=1, device_id=at_inp(d), device_id_type=pl.DeviceIdType.MESH
            )

    for load in loads[1:4]:
        load.wait()
    wo_inverse = build_tables(wo_books, wo_tab)
    wo_scale[...] = wo_scale[...] * wo_inverse

    def unpack_wo(t):
        for u in range(Y):
            block = t * Y + u
            unpack_rows(wo_codes, wo_tab, wo_scale, w1, block, u * n_z + t)

    def unpack_gate(first, last):
        def step(t, carry):
            for u in range(4):
                block = t * 4 + u
                unpack_rows(gate_codes, gate_tab, gate_scale, w2, block, block)
            return carry

        lax.fori_loop(first // 4, last // 4, step, 0)

    unpack_wo(0)

    def relay_features(t, carry):
        tile = rem(z + offset(t, n_z), n_z)
        remote(xt.at[y, z], xt.at[y, tile], a1s, a1r.at[tile], at_z(1)).wait_recv()
        for d in (2, 1, 3):
            a2(t, d).start()
        unpack_wo(t)
        return carry

    lax.fori_loop(1, n_z, relay_features, 0)
    for load in loads[4:]:
        load.wait()
    gate_inverse = build_tables(gate_books, gate_tab)
    gate_scale[...] = gate_scale_flat[...][None, :] * gate_inverse
    residual = remote(res, res_in, rs, rr, {"inp": z, "out": inp * Y + y})

    @pl.when(jnp.logical_not(diagonal))
    def _():
        pl.semaphore_wait(ready, 1)
        residual.start()

    unpack_gate(0, early)

    def project(source):
        lhs = xt[source].reshape(n_z * 64, B)
        start = pl.multiple_of(source * (n_z * 64), n_z * 64)
        return lax.dot_general(
            lhs, w1[pl.ds(start, n_z * 64), :], (((0,), (0,)), ((), ())), preferred_element_type=F32
        )

    acc1[...] = project(y)
    for d in (1, 3, 2):
        source = rem(y + d, Y)
        remote(xt.at[y], xt.at[source], a2s.at[0], a2r.at[source], at_y(d)).wait_recv()
        if d == 2:
            part1[...] = (acc1[...] + project(source)).astype(BF16).reshape(part1.shape)
        else:
            acc1[...] += project(source)

    def column(r):
        return {"inp": z, "out": r * Y + y}

    def b(t):
        r = rem(z + offset(t, n_z), n_z)
        return remote(part1.at[r], in1.at[inp], bs, br, column(r))

    for t in range(n_z - 1, 0, -1):
        b(t).start()

    @pl.when(diagonal)
    def _():
        in1[inp] = part1[z]

    @pl.when(jnp.logical_not(diagonal))
    def _():
        b(0).start()

    most = pl.ds(0, n_z - 1)
    remote(xt.at[y, most], xt.at[y, most], a1s, a1r.at[z], at_z(1)).wait_send()
    for d in range(1, Y):
        remote(xt.at[y], xt.at[y], a2s.at[d], a2r.at[y], at_y(d)).wait_send()
    unpack_gate(early, early + middle)

    @pl.when(diagonal)
    def _():
        res_in[...] = res[...]

    @pl.when(jnp.logical_not(diagonal))
    def _():
        residual.wait_send()
        remote(res, res_in, rs, rr, column(inp)).wait_recv()

    def parts(n):
        return remote(part1.at[pl.ds(0, n)], in1.at[pl.ds(0, n)], bs, br, at_z(1))

    @pl.when(diagonal)
    def _():
        parts(n_inp - 1).wait_recv()

    @pl.when(jnp.logical_not(diagonal))
    def _():
        parts(n_inp).wait_recv()

    total = in1[0].astype(F32)
    for d in range(1, n_inp):
        total = total + in1[d].astype(F32)
    hidden = res_in[...].astype(F32) + total
    gained = hidden * gain[...]
    new = lax.broadcasted_iota(I32, (8, 128), 1)
    order = 64 * (new // 64) + 8 * (new % 8) + (new % 64) // 8
    for n in range(gained.shape[1] // 128):
        columns = slice(n * 128, n * 128 + 128)
        moved = [pick(gained[8 * h : 8 * h + 8, columns], order) for h in range(rows // 8)]
        x2[y, z, :, columns] = jnp.concatenate(moved, axis=0).astype(BF16)

    def c1(t):
        return remote(x2.at[y, z], x2.at[y, z], c1s, c1r.at[z], at_z(offset(t, n_z)))

    def c2(t, d):
        tile = rem(z + offset(t, n_z), n_z)
        return remote(x2.at[y, tile], x2.at[y, tile], c2s.at[d], c2r.at[y], at_y(d))

    for t in range(1, n_z):
        c1(t).start()
    for d in (1, 3, 2):
        c2(0, d).start()

    row = lax.broadcasted_iota(I32, (rows, 128), 0)
    lane = lax.broadcasted_iota(I32, (rows, 128), 1)
    squares = jnp.sum(hidden * hidden, axis=1, keepdims=True)
    squares_in[inp] = jnp.sum(jnp.where(row == lane, squares, 0.0), axis=0, keepdims=True)
    inp_sum = remote(squares_in.at[inp], squares_in.at[inp], qs, qr.at[inp], {"inp": z})
    pl.when(jnp.logical_not(diagonal))(inp_sum.start)
    stream_rows = in1.at[0]
    in1[0] = hidden.astype(BF16)

    def stream(d):
        target = {"inp": rem(inp + d, n_inp), "out": inp * Y + y}
        return remote(stream_rows, stream_ref.at[row_slice(z)], sts, strr, target)

    @pl.when(diagonal)
    def _():
        stream_ref[row_slice(z), :] = hidden.astype(BF16)

    def y_sum(d):
        return remote(squares_y.at[y], squares_y.at[y], ys.at[d], yr.at[y], at_y(d))

    def z_sum(d):
        return remote(squares_all, squares_all, zs.at[d], zr, at_z(d))

    for t in range(1, n_z):
        tile = rem(z + offset(t, n_z), n_z)
        remote(x2.at[y, z], x2.at[y, tile], c1s, c1r.at[tile], at_z(1)).wait_recv()
        for d in (2, 1, 3):
            c2(t, d).start()
    for d in range(1, n_inp):
        stream(d).start()
    pl.when(jnp.logical_not(diagonal))(stream(0).start)

    @pl.when(diagonal)
    def _():
        for d in range(1, n_inp):
            source = rem(inp + d, n_inp)
            remote(
                squares_in.at[inp], squares_in.at[source], qs, qr.at[source], at_inp(d)
            ).wait_recv()
        squares_y[y] = jnp.sum(squares_in[...], axis=0)
        for d in range(1, Y):
            y_sum(d).start()

    unpack_gate(early + middle, early + middle + late)

    depth = x2.shape[3]

    def gate_rows(source):
        return pl.ds(pl.multiple_of(source * depth, depth), depth)

    def arrived(d):
        source = rem(y + d, Y)
        if d:
            remote(x2.at[y], x2.at[source], c2s.at[0], c2r.at[source], at_y(d)).wait_recv()
        return source

    for d in (0, 1, 3):
        source = arrived(d)
        for start, width in blocks:
            columns = pl.ds(start, width)
            product = jnp.dot(
                x2[source].reshape(B, depth), w2[gate_rows(source), columns], preferred_element_type=F32
            ).reshape(n_x, 2, rows, width)
            if d:
                acc2[:, :, :, columns] += product
            else:
                acc2[:, :, :, columns] = product

    def d1(k):
        columns = pl.ds(*blocks[k])
        return remote(
            part2.at[:, :, columns], pair2.at[:, :, columns], d1s.at[k], d1r.at[k],
            {"inp": 2 * x + 1 - core},
        )

    def d2(k, d):
        columns = pl.ds(*blocks[k])
        return remote(
            send2.at[rem(x + d, n_x), :, columns], in2.at[x, :, columns], d2s.at[k, d], d2r.at[k, x],
            {"inp": (rem(x + d, n_x)) * 2 + core},
        )

    source = arrived(2)
    for k, (start, width) in enumerate(blocks):
        columns = pl.ds(start, width)
        acc2[:, :, :, columns] += jnp.dot(
            x2[source].reshape(B, depth), w2[gate_rows(source), columns], preferred_element_type=F32
        ).reshape(n_x, 2, rows, width)
        part2[:, :, columns] = acc2[:, 1 - core, :, columns].astype(BF16)
        d1(k).start()
    for k, (start, width) in enumerate(blocks):
        columns = pl.ds(start, width)
        d1(k).wait_recv()
        both = acc2[:, core, :, columns] + pair2[:, :, columns].astype(F32)
        send2[:, :, columns] = both.astype(BF16)
        for d in (2, 1, 3):
            d2(k, d).start()

    @pl.when(diagonal)
    def _():
        for d in range(1, Y):
            source = rem(y + d, Y)
            remote(squares_y.at[y], squares_y.at[source], ys.at[0], yr.at[source], at_y(d)).wait_recv()
        squares_all[...] = jnp.sum(squares_y[...], axis=0)
        for d in range(1, n_z):
            z_sum(d).start()

    def streams(n):
        there = stream_ref.at[pl.ds(0, n * rows)]
        return remote(there, there, sts, strr, at_z(1))

    @pl.when(jnp.logical_not(diagonal))
    def _():
        streams(n_inp).wait_recv()
        streams(n_inp).wait_send()
        parts(n_inp).wait_send()
        inp_sum.wait_send()

    @pl.when(diagonal)
    def _():
        streams(n_inp - 1).wait_recv()
        streams(n_inp - 1).wait_send()
        parts(n_inp - 1).wait_send()
        for d in range(1, Y):
            y_sum(d).wait_send()

    remote(x2.at[y, most], x2.at[y, most], c1s, c1r.at[z], at_z(1)).wait_send()
    for d in range(1, Y):
        remote(x2.at[y], x2.at[y], c2s.at[d], c2r.at[y], at_y(d)).wait_send()

    @pl.when(diagonal)
    def _():
        for d in range(1, n_z):
            z_sum(d).wait_send()

    @pl.when(jnp.logical_not(diagonal))
    def _():
        remote(squares_all, squares_all, zs.at[0], zr, at_z(1)).wait_recv()

    mean = squares_all[...] * (1.0 / (depth * Y * n_z))
    mean = jnp.sum(jnp.where(row == lane, mean, 0.0), axis=1, keepdims=True)
    factor = lax.rsqrt(mean + EPS)

    for k, (start, width) in enumerate(blocks):
        columns = pl.ds(start, width)
        total = acc2[x, core, :, columns] + pair2[x, :, columns].astype(F32)
        for d in (1, 3, 2):
            source = rem(x + d, n_x)
            remote(
                send2.at[x, :, columns], in2.at[source, :, columns], d2s.at[k, 0], d2r.at[k, source],
                {"inp": source * 2 + core},
            ).wait_recv()
            total = total + in2[source, :, columns].astype(F32)
        gate_ref[:, columns] = (total * factor).astype(BF16)
        d1(k).wait_send()
        for d in range(1, n_x):
            d2(k, d).wait_send()


def place(stream, gate, stream_out, gate_out, sem):
    copies = [
        pltpu.make_async_copy(stream, stream_out, sem.at[0]),
        pltpu.make_async_copy(gate, gate_out, sem.at[1]),
    ]
    for copy in copies:
        copy.start()
    for copy in copies:
        copy.wait()


def per_device(
    attention, residual, wo_codes, wo_books, wo_scale, norm_gain, gate_codes, gate_books, gate_scale
):
    n_inp, n_out = lax.axis_size("inp"), lax.axis_size("out")
    n_z, n_x = n_out // Y, n_inp // 2
    rows = B // n_inp
    width, gate_width = wo_codes.shape[2], gate_codes.shape[2]
    depth = wo_codes.shape[1] * GROUP
    blocks = ((0, 1664),)
    vmem = pl.BlockSpec(memory_space=pltpu.VMEM)
    hbm = pl.BlockSpec(memory_space=pltpu.HBM)
    dma = pltpu.SemaphoreType.DMA
    args = (
        attention.T, residual, wo_codes, jnp.swapaxes(wo_books, 1, 2), wo_scale[None, :],
        norm_gain.reshape(n_out, 1, width), gate_codes, jnp.swapaxes(gate_books, 1, 2), gate_scale,
    )
    held = [pltpu.VMEM(a.shape, a.dtype) for a in args]
    held[1] = pltpu.VMEM((rows, width), BF16)
    held[5] = pltpu.VMEM((1, width), F32)
    stream, gate = pl.pallas_call(
        functools.partial(kernel, blocks=blocks, early=8, middle=16, late=8),
        out_shape=(
            jax.ShapeDtypeStruct((B, width), BF16),
            jax.ShapeDtypeStruct((rows, gate_width), BF16),
        ),
        in_specs=[hbm] * 9,
        out_specs=(vmem, vmem),
        scratch_shapes=[
            *held,
            pltpu.VMEM((1, gate_width), F32),
            pltpu.VMEM((2, 4, 2, 8, 128), I32),
            pltpu.VMEM((2, 4, 2, 8, 128), I32),
            pltpu.VMEM((Y, n_z, 64, B), BF16),
            pltpu.VMEM((depth, width), BF16),
            pltpu.VMEM((B, width), F32),
            pltpu.VMEM((n_inp, rows, width), BF16),
            pltpu.VMEM((n_inp, rows, width), BF16),
            pltpu.VMEM((Y, n_z, rows, width), BF16),
            pltpu.VMEM((depth, gate_width), BF16),
            pltpu.VMEM((n_x, 2, rows, gate_width), F32),
            pltpu.VMEM((n_x, rows, gate_width), BF16),
            pltpu.VMEM((n_x, rows, gate_width), BF16),
            pltpu.VMEM((n_x, rows, gate_width), BF16),
            pltpu.VMEM((n_x, rows, gate_width), BF16),
            pltpu.VMEM((n_inp, 1, 128), F32),
            pltpu.VMEM((Y, 1, 128), F32),
            pltpu.VMEM((1, 128), F32),
            pltpu.VMEM((rows, width), BF16),
            dma((9,)), pltpu.SemaphoreType.REGULAR,
            dma, dma((n_z,)),
            dma((Y,)), dma((Y,)),
            dma, dma,
            dma, dma,
            dma, dma,
            dma, dma((n_z,)),
            dma((Y,)), dma((Y,)),
            dma, dma((n_inp,)),
            dma((Y,)), dma((Y,)),
            dma((n_z,)), dma,
            dma((len(blocks),)), dma((len(blocks),)),
            dma((len(blocks), n_x)), dma((len(blocks), n_x)),
        ],
        compiler_params=pltpu.CompilerParams(
            collective_id=0, has_side_effects=True, vmem_limit_bytes=48 << 20
        ),
        name="step",
    )(*[pltpu.with_memory_space_constraint(a, pltpu.HBM) for a in args])
    return pl.pallas_call(
        place,
        out_shape=(
            jax.ShapeDtypeStruct(stream.shape, BF16),
            jax.ShapeDtypeStruct(gate.shape, BF16),
        ),
        in_specs=[vmem, vmem],
        out_specs=(hbm, hbm),
        scratch_shapes=[dma((2,))],
        compiler_params=pltpu.CompilerParams(vmem_limit_bytes=4 << 20),
        name="place",
    )(stream, gate)


def solution(mesh):
    placed = (
        P(None, ("inp", "out")),
        P(None, "out"),
        P(None, "inp", "out"),
        P(),
        P("out"),
        P(),
        P(None, "inp", "out"),
        P(),
        P("out"),
    )
    return jax.shard_map(
        per_device,
        mesh=mesh,
        in_specs=placed,
        out_specs=(P(None, "out"), P("inp", "out")),
        check_vma=False,
    )
```
